128 devices in a mesh: rep: 16 (over x_hi, y, core), tp: 8 (over z, x_lo).
Axes of the slice: x: 4 (x_hi: 2, x_lo: 2; x = x_hi * 2 + x_lo), y: 4, z: 4, core: 2. Of those that a mesh axis runs over, the one named last changes fastest.
Arguments:
- residual: bfloat16 [65536, 8192], P(('rep', 'tp')), may hold values from -24 to 24
- norm_gain: bfloat16 [8192], P(('rep', 'tp')), may hold values from 0.5 to 1.5
- value_weight: bfloat16 [8192, 512], P(('rep', 'tp')), may hold values from -0.0625 to 0.0625
- value_cot: bfloat16 [65536, 512], P(('rep', 'tp')), may hold values from -12 to 12
- trainee_logp: float32 [65536], P(('rep', 'tp')), may hold values from -40 to -8
- ref_shard_max: float32 [8, 65536], P('tp', 'rep'), may hold values from 90 to 120
- ref_shard_sum: float32 [8, 65536], P('tp', 'rep'), may hold values from 1 to 1000
- ref_target_logit: float32 [8, 65536], P('tp', 'rep'), may hold values from 80 to 120
- target_ids: int32 [65536], P('rep'), may hold values from 0 to 128255
- lengths: int32 [16], replicated, may hold values from 2048 to 4096, as said below
Outputs:
- value_proj: bfloat16 [65536, 512], P(('rep', 'tp'))
- resid_grad: bfloat16 [65536, 8192], P(('rep', 'tp'))
- weight_grad: float32 [8192, 512], P(('rep', 'tp'))
- gain_grad: float32 [8192], P(('rep', 'tp'))
The draws below stay inside these ranges and needn't reach their ends.
Inputs may be any that keep to these rules, and one draw needn't show every extreme that they name: `lengths`: one sequence has all 4096 tokens live and one has 2048.
All inputs are finite; a program needn't handle non-finite values.
Results may differ from the reference program's by a relative error of at most 0.009.
Values may be sent and summed in bfloat16 or wider, within the bound.
A program may use at most 192 MiB of HBM per device.

```python
import math
import jax
import jax.numpy as jnp
from jax import lax

D = 8192
HV = 512
VOCAB = 128256
SEQ = 4096
SEQS = 16
TOKENS = 65536
N_TP = 8


def draw_lengths(key, part):
    first_key, second_key = jax.random.split(jax.random.fold_in(key, 7))
    drawn = jax.random.randint(first_key, (SEQS,), SEQ // 2, SEQ + 1)
    order = jax.random.permutation(second_key, SEQS)
    drawn = drawn.at[order[0]].set(SEQ)
    drawn = drawn.at[order[1]].set(SEQ // 2)
    return drawn.astype(jnp.int32)


def with_ends(result, rng, low, largest):
    place = [jax.random.randint(jax.random.fold_in(rng, axis), (), 0, length) for axis, length in enumerate(result.shape)]
    longest = result.shape.index(max(result.shape))
    neighbour = place[:longest] + [(place[longest] + 1) % result.shape[longest]] + place[longest + 1:]
    return result.at[tuple(place)].set(low).at[tuple(neighbour)].set(largest)


def spiked(entries, own_key, source, target, blocks, factor):
    def block_of(dim):
        return (jnp.arange(entries.shape[dim]) // (entries.shape[dim] // blocks)).reshape((-1,) + (1,) * (entries.ndim - 1 - dim))

    first = jax.random.permutation(own_key, blocks)[block_of(target)]
    far = (block_of(target) + blocks // 2) % blocks
    return jnp.where((block_of(source) == first) | (block_of(source) == far), factor * entries, entries)


def shard_levels(own_key, shape, shards, least, top_value):
    def one(axis_at, shards_of):
        steps = jax.random.uniform(jax.random.fold_in(jax.random.fold_in(own_key, 6), axis_at), (shards_of,), jnp.float32, least / len(shards), top_value / len(shards))
        return jnp.repeat(jnp.exp(steps), shape[axis_at] // shards_of).reshape((-1,) + (1,) * (len(shape) - axis_at - 1))

    level = one(*shards[0])
    for cut in shards[1:]:
        level = level * one(*cut)
    return level


def centred(stream_key, shape, deviation, bound, shards=(), held_as=jnp.bfloat16):
    level = shard_levels(stream_key, shape, shards, -0.22, 0.18) if shards else 1.0
    array = jax.random.normal(stream_key, shape, jnp.float32) * deviation * level
    return jnp.minimum(jnp.maximum(array, -bound), bound).astype(held_as)


def gaussian_with(rng, extent, scale, reach, cuts, heavy, kind=jnp.bfloat16):
    values = scale * jax.random.normal(rng, extent, jnp.float32)
    if cuts:
        values = values * shard_levels(rng, extent, cuts, -0.22, 0.18)
    return jnp.clip(spiked(values, jax.random.fold_in(rng, 3), *heavy), -reach, reach).astype(kind)


def setup_inputs(seed: int = 0) -> dict:
    key_list = jax.random.split(jax.random.key(seed), 11)
    residual = gaussian_with(key_list[0], (TOKENS, D), 1.0, 24.0, ((0, 128),), (0, 1, 128, 5.5))
    norm_gain = jnp.clip(1.0 + 0.1 * jax.random.normal(key_list[1], (D,), jnp.float32), 0.5, 1.5).astype(jnp.bfloat16)
    value_weight = centred(key_list[2], (D, HV), D ** -0.5, 0.0625, ((0, 128),))
    value_cot = centred(key_list[3], (TOKENS, HV), 2.0, 12.0, ((0, 128),))
    trainee_logp = jnp.clip(-40.0 + 32.0 * jax.random.uniform(key_list[4], (TOKENS,), jnp.float32) ** shard_levels(key_list[4], (TOKENS,), ((0, 128),), -0.2, 0.2), -40.0, -8.0)
    ref_shard_max = jnp.clip(90.0 + 30.0 * jax.random.uniform(key_list[5], (N_TP, TOKENS), jnp.float32) ** shard_levels(key_list[5], (N_TP, TOKENS), ((0, 8), (1, 16)), -0.2, 0.2), 90.0, 120.0)
    ref_shard_sum = jnp.clip(jnp.exp(math.log(1000.0) - 6.9077553 * jax.random.uniform(key_list[6], (N_TP, TOKENS), jnp.float32) ** shard_levels(key_list[6], (N_TP, TOKENS), ((0, 8), (1, 16)), -0.2, 0.2)), 1.0, 1000.0)
    ref_target_logit = jnp.clip(80.0 + 40.0 * jax.random.uniform(key_list[7], (N_TP, TOKENS), jnp.float32) ** shard_levels(key_list[7], (N_TP, TOKENS), ((0, 8), (1, 16)), -0.2, 0.2), 80.0, 120.0)
    target_ids = with_ends(jax.random.randint(key_list[8], (TOKENS,), 0, VOCAB), jax.random.fold_in(key_list[8], 1), 0, VOCAB - 1).astype(jnp.int32)
    lengths = draw_lengths(jax.random.fold_in(key_list[10], 71), 0)
    return {"residual": residual, "norm_gain": norm_gain, "value_weight": value_weight, "value_cot": value_cot, "trainee_logp": trainee_logp, "ref_shard_max": ref_shard_max, "ref_shard_sum": ref_shard_sum, "ref_target_logit": ref_target_logit, "target_ids": target_ids, "lengths": lengths}


EPS = 1e-05
BETA = 0.5

def reference(residual, norm_gain, value_weight, value_cot, trainee_logp, ref_shard_max, ref_shard_sum, ref_target_logit, target_ids, lengths):
    top_max = lax.optimization_barrier(jnp.max(ref_shard_max, axis=0))
    sum_exp = lax.optimization_barrier(jnp.sum(ref_shard_sum * jnp.exp(ref_shard_max - top_max[None, :]), axis=0))
    owner_shard = target_ids // (VOCAB // N_TP)
    shard_ids = jnp.arange(N_TP, dtype=jnp.int32)
    picked = lax.optimization_barrier(jnp.sum(jnp.where(owner_shard[None, :] == shard_ids[:, None], ref_target_logit, jnp.zeros_like(ref_target_logit)), axis=0))
    ref_logp = picked - top_max - jnp.log(sum_exp)
    positions = jnp.arange(SEQ, dtype=jnp.int32)
    live_rows = (positions[None, :] < lengths[:, None]).astype(jnp.float32)
    token_diff = (trainee_logp - ref_logp).reshape(SEQS, SEQ) * live_rows
    seq_delta = lax.optimization_barrier(jnp.sum(token_diff, axis=1)) / lengths.astype(jnp.float32)
    seq_weight = 2.0 * jax.nn.sigmoid(BETA * seq_delta) / SEQS
    row_scale = live_rows * seq_weight[:, None]
    gain_wide = norm_gain.astype(jnp.float32)

    def one_sequence(carry, inputs):
        weight_acc, gain_acc = carry
        resid_block, cot_block, scale_block = inputs
        resid_wide = resid_block.astype(jnp.float32)
        inv_rms = lax.rsqrt(lax.optimization_barrier(jnp.mean(resid_wide * resid_wide, axis=1, keepdims=True)) + EPS)
        unit_rows = resid_wide * inv_rms
        normed = (unit_rows * gain_wide).astype(jnp.bfloat16)
        value_proj = jnp.dot(normed, value_weight, preferred_element_type=jnp.float32).astype(jnp.bfloat16)
        scaled = (scale_block[:, None] * cot_block.astype(jnp.float32)).astype(jnp.bfloat16)
        normed_grad = jnp.dot(scaled, value_weight.T, preferred_element_type=jnp.float32)
        unit_grad = normed_grad * gain_wide
        project_mean = lax.optimization_barrier(jnp.mean(unit_grad * unit_rows, axis=1, keepdims=True))
        resid_grad = (inv_rms * (unit_grad - unit_rows * project_mean)).astype(jnp.bfloat16)
        weight_acc = weight_acc + jnp.dot(normed.T, scaled, preferred_element_type=jnp.float32)
        gain_acc = gain_acc + lax.optimization_barrier(jnp.sum(normed_grad * unit_rows, axis=0))
        return ((weight_acc, gain_acc), (value_proj, resid_grad))
    start_carry = (jnp.zeros((D, HV), jnp.float32), jnp.zeros((D,), jnp.float32))
    stacked = (residual.reshape(SEQS, SEQ, D), value_cot.reshape(SEQS, SEQ, HV), row_scale)
    (weight_grad, gain_grad), (value_rows, resid_rows) = lax.scan(one_sequence, start_carry, stacked)
    return (value_rows.reshape(TOKENS, HV), resid_rows.reshape(TOKENS, D), weight_grad, gain_grad)
```

```python
import jax
import jax.numpy as jnp
from jax import lax
from jax.experimental import pallas as pl
from jax.experimental.pallas import tpu as pltpu
from jax.sharding import PartitionSpec as P

VOCAB = 128256
EPS = 1e-05
BETA = 0.5
MESH = pl.DeviceIdType.MESH

PIECES = (
    ((0, 1, 2), ((0, 64, 0, 128), (0, 32, 384, 128))),
    ((1, 2, 0), ((0, 64, 128, 128), (32, 16, 384, 128))),
    ((2, 0, 1), ((0, 64, 256, 128), (48, 16, 384, 128))),
)
CUBE = (2, 4, 4, 2)


def where_am_i():
    rep, tp = lax.axis_index("rep"), lax.axis_index("tp")
    core = lax.rem(rep, 2)
    y = lax.rem(rep // 2, 4)
    x = (rep // 8) * 2 + lax.rem(tp, 2)
    z = tp // 2
    return (x, y, z), core


def device(c, core):
    x, y, z = c
    return ((x // 2) * 8 + y * 2 + core, z * 2 + lax.rem(x, 2))


def moved(c, axis, by):
    return c[:axis] + (lax.rem(c[axis] + 4 + by, 4),) + c[axis + 1 :]


def put(c, axis, value):
    return c[:axis] + (value,) + c[axis + 1 :]


def part(ref, c, rect, lead=()):
    x, y, z = c
    every = slice(None)
    xh, xl = (every, every) if x is None else (x // 2, lax.rem(x, 2))
    r0, nr, c0, nc = rect
    return ref.at[
        lead
        + (
            xh,
            every if y is None else y,
            every if z is None else z,
            xl,
            pl.ds(r0, nr),
            pl.ds(c0, nc),
        )
    ]


class Wire:
    def __init__(self, send_sem, recv_sem):
        self.send_sem, self.recv_sem, self.count, self.all = send_sem, recv_sem, 0, []

    def copy(self, src, dst, to):
        k = self.count
        self.count += 1
        made = pltpu.make_async_remote_copy(
            src_ref=src,
            dst_ref=dst,
            send_sem=self.send_sem.at[k],
            recv_sem=self.recv_sem.at[k],
            device_id=to,
            device_id_type=MESH,
        )
        self.all.append(made)
        return made

    def copies(self, src, src_c, dst, dst_c, rects, to, lead=()):
        return [
            self.copy(part(src, src_c, r, lead), part(dst, dst_c, r, lead), to)
            for r in rects
        ]


def start(copies):
    for c in copies:
        c.start()


def recv(copies):
    for c in copies:
        c.wait_recv()


def greet(devices):
    barrier = pltpu.get_barrier_semaphore()
    for d in devices:
        pl.semaphore_signal(barrier, inc=1, device_id=d, device_id_type=MESH)
    pl.semaphore_wait(barrier, len(devices))


def neighbours(me, core):
    near = [device(moved(me, a, s), core) for a in range(3) for s in (1, -1)]
    return near + [device(me, 1 - core)]


GATHER_COPIES = 3 * 2 * 18 + 3 * 2 * 4


class Gather:
    def __init__(self, wire, full, me, core):
        d = 1 - 2 * core
        self.full, self.me, self.core = full, me, core
        partner = device(me, 1 - core)
        self.plan = []
        for (a1, a2, a3), rects in PIECES:
            t = {}

            def make(name, c, to):
                t[name] = wire.copies(full, c, full, c, rects, to, (core,))

            up = [device(moved(me, a, d), core) for a in (a1, a2, a3)]
            down = [device(moved(me, a, -d), core) for a in (a1, a2, a3)]
            make("1p", me, up[0])
            make("1m", me, down[0])
            make("1f", moved(me, a1, -d), up[0])
            row = put(me, a1, None)
            make("2p", row, up[1])
            make("2m", row, down[1])
            make("2f", moved(row, a2, -d), up[1])
            for j, by in enumerate((0, -d, d, 2)):
                line = moved(row, a2, by)
                make(f"3p{j}", line, up[2])
                make(f"3m{j}", line, down[2])
                make(f"3f{j}", moved(line, a3, -d), up[2])
            slab = put(row, a2, None)
            for j, by in enumerate((0, -d, d, 2)):
                make(f"x{j}", moved(slab, a3, by), partner)
            self.plan.append(t)

    def start(self):
        for t in self.plan:
            start(t["1p"] + t["1m"])

    def step1(self):
        for t in self.plan:
            recv(t["1p"])
            start(t["1f"])

    def step2(self):
        for t in self.plan:
            recv(t["1m"])
            recv(t["1f"])
            start(t["2p"] + t["2m"] + t["3p0"] + t["3m0"])

    def step3(self):
        for t in self.plan:
            recv(t["2p"])
            start(t["2f"] + t["3p1"] + t["3m1"])

    def step4(self):
        for t in self.plan:
            recv(t["2m"])
            start(t["3p2"] + t["3m2"])

    def step5(self):
        for t in self.plan:
            recv(t["2f"])
            start(t["3p3"] + t["3m3"] + t["x0"])

    def step6(self, j):
        for t in self.plan:
            recv(t[f"3p{j}"])
            start(t[f"3f{j}"])

    def step7(self):
        for t in self.plan:
            start(t["x1"])
        for t in self.plan:
            for j in range(4):
                recv(t[f"3m{j}"])
            start(t["x2"])

    def step8(self):
        for t in self.plan:
            for j in range(4):
                recv(t[f"3f{j}"])
            start(t["x3"])

    def step9(self):
        for j in range(4):
            for t in self.plan:
                recv(t[f"x{j}"])

    def run(self):
        self.start()
        self.step1()
        self.step2()
        self.step3()
        self.step4()
        self.step5()
        for j in range(4):
            self.step6(j)
        self.step7()
        self.step8()
        self.step9()


REDUCE_COPIES = 3 * 2 * 18


class Reduce:
    def __init__(self, wire, total, land, me, core):
        d = 1 - 2 * core
        self.total, self.land, self.me = total, land, me
        self.plan = []
        for (a1, a2, a3), rects in PIECES:
            t = {"rects": rects, "axes": (a1, a2, a3)}

            def make(name, src_c, dst_c, to):
                t[name] = wire.copies(total, src_c, land, dst_c, rects, to)

            up = [device(moved(me, a, d), core) for a in (a1, a2, a3)]
            down = [device(moved(me, a, -d), core) for a in (a1, a2, a3)]
            row = put(me, a1, None)
            t["lines"] = []
            for j, by in enumerate((2, -d, d, 0)):
                line = moved(row, a2, by)
                t["lines"].append(line)
                make(f"3x{j}", moved(line, a3, 2), moved(line, a3, 2), up[2])
                make(f"3m{j}", moved(line, a3, -d), moved(line, a3, 2), down[2])
                make(f"3p{j}", moved(line, a3, d), moved(line, a3, d), up[2])
            far = moved(row, a3, 2)
            make("2x", moved(row, a2, 2), moved(far, a2, 2), up[1])
            make("2m", moved(row, a2, -d), moved(far, a2, 2), down[1])
            make("2p", moved(row, a2, d), moved(far, a2, d), up[1])
            spot = moved(moved(me, a3, 2), a2, 2)
            make("1x", moved(me, a1, 2), moved(spot, a1, 2), up[0])
            make("1m", moved(me, a1, -d), moved(spot, a1, 2), down[0])
            make("1p", moved(me, a1, d), moved(spot, a1, d), up[0])
            t["d"], t["row"], t["far"], t["spot"] = d, row, far, spot
            self.plan.append(t)

    def add(self, t, where, sources):
        a1 = t["axes"][0]

        def one(c, sources_c):
            for r in t["rects"]:
                value = part(self.total, c, r)[...].astype(jnp.float32)
                for s in sources_c:
                    value = value + part(self.land, s, r)[...].astype(jnp.float32)
                part(self.total, c, r)[...] = value.astype(jnp.bfloat16)

        if where[a1] is None:

            @pl.loop(0, 4)
            def _(i):
                one(put(where, a1, i), [put(s, a1, i) for s in sources])

        else:
            one(where, sources)

    def start(self):
        for j in range(4):
            for t in self.plan:
                start(t[f"3x{j}"] + t[f"3m{j}"])

    def relay3(self, j):
        for t in self.plan:
            recv(t[f"3x{j}"])
            up = moved(t["lines"][j], t["axes"][2], t["d"])
            self.add(t, up, [up])
            start(t[f"3p{j}"])

    def close3(self, j):
        for t in self.plan:
            recv(t[f"3p{j}"])
            recv(t[f"3m{j}"])
            line, a3 = t["lines"][j], t["axes"][2]
            self.add(t, line, [line, moved(line, a3, -t["d"])])
            if j == 0:
                start(t["2x"])
            if j == 1:
                start(t["2m"])

    def relay2(self):
        for t in self.plan:
            recv(t["2x"])
            a2 = t["axes"][1]
            self.add(t, moved(t["row"], a2, t["d"]), [moved(t["far"], a2, t["d"])])
            start(t["2p"])

    def close2(self):
        for t in self.plan:
            recv(t["2p"])
            recv(t["2m"])
            a2 = t["axes"][1]
            self.add(t, t["row"], [t["far"], moved(t["far"], a2, -t["d"])])
            start(t["1x"] + t["1m"])

    def relay1(self):
        for t in self.plan:
            recv(t["1x"])
            a1 = t["axes"][0]
            self.add(t, moved(self.me, a1, t["d"]), [moved(t["spot"], a1, t["d"])])
            start(t["1p"])

    def close1(self, out):
        for t in self.plan:
            recv(t["1p"])
            recv(t["1m"])
            a1, d, spot = t["axes"][0], t["d"], t["spot"]
            for r in t["rects"]:
                value = part(self.total, self.me, r)[...].astype(jnp.float32)
                for s in (spot, moved(spot, a1, -d)):
                    value = value + part(self.land, s, r)[...].astype(jnp.float32)
                out[pl.ds(r[0], r[1]), pl.ds(r[2], r[3])] = value

    def run(self, out):
        self.start()
        for j in range(4):
            self.relay3(j)
        for j in range(3):
            self.close3(j)
        self.relay2()
        self.close3(3)
        self.close2()
        self.relay1()
        self.close1(out)


def tp_peers():
    rep, tp = lax.axis_index("rep"), lax.axis_index("tp")
    return [(rep, lax.rem(tp + k, 8)) for k in range(1, 8)]


def gather_kernel(
    w_ref, gain_ref, smax_ref, ssum_ref, starg_ref, ids_ref, logp_ref, len_ref,
    full_ref, seq_ref,
    stat_out, stat_in, part_out, part_in, send_sem, recv_sem,
    st_send, st_recv, pt_send, pt_recv,
):
    me, core = where_am_i()
    rep, tp = lax.axis_index("rep"), lax.axis_index("tp")
    x, y, z = me
    w = w_ref[...].astype(jnp.float32) * gain_ref[...].astype(jnp.float32)
    full_ref[core, x // 2, y, z, lax.rem(x, 2)] = w.astype(jnp.bfloat16)
    width = VOCAB // 8
    ids = ids_ref[...]
    mine = (ids >= tp * width) & (ids < (tp + 1) * width)
    owned = jnp.where(mine, starg_ref[...], 0.0)
    for k in range(8):
        cut = slice(k * 512, (k + 1) * 512)
        stat_out[k, :, 0:512] = smax_ref[:, cut]
        stat_out[k, :, 512:1024] = ssum_ref[:, cut]
        stat_out[k, :, 1024:1536] = owned[:, cut]
    peers = tp_peers()
    near = neighbours(me, core)
    greet(near + peers)
    wire = Wire(send_sem, recv_sem)
    gather = Gather(wire, full_ref, me, core)
    gather.start()
    stats = [
        pltpu.make_async_remote_copy(
            src_ref=stat_out.at[to[1]], dst_ref=stat_in.at[tp],
            send_sem=st_send.at[k], recv_sem=st_recv.at[k],
            device_id=to, device_id_type=MESH,
        )
        for k, to in enumerate(peers)
    ]
    start(stats)
    stat_in[tp] = stat_out[tp]
    gather.step1()
    gather.step2()
    recv(stats)
    got = [stat_in[k] for k in range(8)]
    top = got[0][:, 0:512]
    for g in got[1:]:
        top = jnp.maximum(top, g[:, 0:512])
    total = jnp.zeros_like(top)
    picked = jnp.zeros_like(top)
    for g in got:
        total = total + g[:, 512:1024] * jnp.exp(g[:, 0:512] - top)
        picked = picked + g[:, 1024:1536]
    ref_logp = picked - top - jnp.log(total)
    length = len_ref[0, rep]
    spot = tp * 512 + lax.broadcasted_iota(jnp.int32, (1, 512), 1)
    live = (spot < length).astype(jnp.float32)
    local = jnp.sum(live * (logp_ref[...] - ref_logp), axis=1, keepdims=True)
    part_out[...] = jnp.broadcast_to(local, (8, 128))
    shares = [
        pltpu.make_async_remote_copy(
            src_ref=part_out, dst_ref=part_in.at[tp],
            send_sem=pt_send.at[k], recv_sem=pt_recv.at[k],
            device_id=to, device_id_type=MESH,
        )
        for k, to in enumerate(peers)
    ]
    start(shares)
    part_in[tp] = part_out[...]
    gather.step3()
    gather.step4()
    gather.step5()
    recv(shares)
    seq_total = part_in[0]
    for k in range(1, 8):
        seq_total = seq_total + part_in[k]
    delta = seq_total / jnp.full((8, 128), length, jnp.int32).astype(jnp.float32)
    seq_ref[...] = 2.0 * jax.nn.sigmoid(BETA * delta) / 16.0
    for j in range(4):
        gather.step6(j)
    gather.step7()
    gather.step8()
    gather.step9()
    for c in wire.all + stats + shares:
        c.wait_send()


def reduce_kernel(g_ref, out_ref, total, land, cross, send_sem, recv_sem, x_send, x_recv, own_sem):
    me, core = where_am_i()
    greet(neighbours(me, core))
    partner = device(me, 1 - core)
    far = [
        pltpu.make_async_remote_copy(
            src_ref=g_ref.at[h, :, 1 - core], dst_ref=cross.at[h],
            send_sem=x_send.at[h], recv_sem=x_recv.at[h],
            device_id=partner, device_id_type=MESH,
        )
        for h in range(2)
    ]
    start(far)
    own = [
        pltpu.make_async_copy(g_ref.at[h, :, core], total.at[h], own_sem.at[h])
        for h in range(2)
    ]
    start(own)
    wire = Wire(send_sem, recv_sem)
    reduce = Reduce(wire, total, land, me, core)
    for h in range(2):
        own[h].wait()
        far[h].wait_recv()

        @pl.loop(0, 32)
        def _(i):
            at = (h, i // 8, lax.rem(i // 2, 4), lax.rem(i, 2))
            value = total[at].astype(jnp.float32) + cross[at].astype(jnp.float32)
            total[at] = value.astype(jnp.bfloat16)

    reduce.run(out_ref)
    for c in wire.all + far:
        c.wait_send()


def gather_all(w, gain, smax, ssum, starg, ids, logp, lengths):
    vmem = pl.BlockSpec(memory_space=pltpu.VMEM)
    dma = pltpu.SemaphoreType.DMA
    return pl.pallas_call(
        gather_kernel,
        out_shape=(
            jax.ShapeDtypeStruct((2,) + CUBE + (64, 512), jnp.bfloat16),
            jax.ShapeDtypeStruct((8, 128), jnp.float32),
        ),
        in_specs=[vmem] * 7 + [pl.BlockSpec(memory_space=pltpu.SMEM)],
        out_specs=(vmem, vmem),
        scratch_shapes=[
            pltpu.VMEM((8, 1, 1536), jnp.float32),
            pltpu.VMEM((8, 1, 1536), jnp.float32),
            pltpu.VMEM((8, 128), jnp.float32),
            pltpu.VMEM((8, 8, 128), jnp.float32),
            dma((GATHER_COPIES + 24,)),
            dma((GATHER_COPIES + 24,)),
            dma((7,)), dma((7,)), dma((7,)), dma((7,)),
        ],
        compiler_params=pltpu.CompilerParams(collective_id=0, has_side_effects=True),
        name="gather",
    )(w, gain, smax, ssum, starg, ids, logp, lengths)


def reduce_all(g):
    dma = pltpu.SemaphoreType.DMA
    return pl.pallas_call(
        reduce_kernel,
        out_shape=jax.ShapeDtypeStruct((64, 512), jnp.float32),
        in_specs=[pl.BlockSpec(memory_space=pl.ANY)],
        out_specs=pl.BlockSpec(memory_space=pltpu.VMEM),
        scratch_shapes=[
            pltpu.VMEM(CUBE + (64, 512), jnp.bfloat16),
            pltpu.VMEM(CUBE + (64, 512), jnp.bfloat16),
            pltpu.VMEM(CUBE + (64, 512), jnp.bfloat16),
            dma((REDUCE_COPIES,)),
            dma((REDUCE_COPIES,)),
            dma((2,)), dma((2,)), dma((2,)),
        ],
        compiler_params=pltpu.CompilerParams(collective_id=1, has_side_effects=True),
        name="reduce",
    )(g)


def per_device(
    residual, norm_gain, value_weight, value_cot, trainee_logp,
    ref_shard_max, ref_shard_sum, ref_target_logit, target_ids, lengths,
):
    rows, d_model = residual.shape
    tp, rep = lax.axis_index("tp"), lax.axis_index("rep")
    full, seq = gather_all(
        value_weight,
        norm_gain.reshape(-1, 1),
        ref_shard_max, ref_shard_sum, ref_target_logit,
        target_ids.reshape(1, -1),
        trainee_logp.reshape(1, -1),
        lengths.reshape(1, -1),
    )
    full = full.reshape(2, 2, 4, 512, 512)
    weight = jnp.transpose(full, (1, 2, 0, 3, 4)).reshape(d_model, 512)
    seq_weight = seq[0, 0]
    wide = residual.astype(jnp.float32)
    inv_rms = lax.rsqrt(jnp.mean(wide * wide, axis=1, keepdims=True) + EPS)
    seq_length = lax.dynamic_index_in_dim(lengths, rep, keepdims=False)
    live = ((tp * rows + jnp.arange(rows, dtype=jnp.int32)) < seq_length).astype(jnp.float32)[:, None]
    cot = value_cot.astype(jnp.float32)
    inner = (inv_rms * live * cot).astype(jnp.bfloat16)
    g = lax.dot_general(residual, inner, (((0,), (0,)), ((), ())), preferred_element_type=jnp.float32)
    g = (g * seq_weight).astype(jnp.bfloat16).reshape(2, 4, 2, 4, 2, 64, 512)
    value = inv_rms * jnp.dot(residual, weight, preferred_element_type=jnp.float32)
    scale = live * seq_weight
    mean = scale * jnp.sum(cot * value, axis=1, keepdims=True) / d_model
    back = lax.dot_general(value_cot, weight, (((1,), (1,)), ((), ())), preferred_element_type=jnp.float32)
    resid_grad = (inv_rms * (scale * back - wide * (inv_rms * mean))).astype(jnp.bfloat16)
    total = reduce_all(g)
    weight_grad = total * norm_gain.astype(jnp.float32)[:, None]
    gain_grad = jnp.sum(total * value_weight.astype(jnp.float32), axis=1)
    return value.astype(jnp.bfloat16), resid_grad, weight_grad, gain_grad


def solution(mesh):
    placed = (
        P(("rep", "tp"), None),
        P(("rep", "tp")),
        P(("rep", "tp"), None),
        P(("rep", "tp"), None),
        P(("rep", "tp")),
        P("tp", "rep"),
        P("tp", "rep"),
        P("tp", "rep"),
        P("rep"),
        P(),
    )
    return jax.shard_map(
        per_device,
        mesh=mesh,
        in_specs=placed,
        out_specs=(
            P(("rep", "tp"), None),
            P(("rep", "tp"), None),
            P(("rep", "tp"), None),
            P(("rep", "tp")),
        ),
        check_vma=False,
    )
```

```python
import jax
import jax.numpy as jnp
from jax import lax
from jax.experimental import pallas as pl
from jax.experimental.pallas import tpu as pltpu
from jax.sharding import PartitionSpec as P

VOCAB = 128256
EPS = 1e-05
BETA = 0.5
MESH = pl.DeviceIdType.MESH

PIECES = (
    ((0, 1, 2), ((0, 64, 0, 128), (0, 32, 384, 128))),
    ((1, 2, 0), ((0, 64, 128, 128), (32, 16, 384, 128))),
    ((2, 0, 1), ((0, 64, 256, 128), (48, 16, 384, 128))),
)
CUBE = (2, 4, 4, 2)


def where_am_i():
    rep, tp = lax.axis_index("rep"), lax.axis_index("tp")
    core = lax.rem(rep, 2)
    y = lax.rem(rep // 2, 4)
    x = (rep // 8) * 2 + lax.rem(tp, 2)
    z = tp // 2
    return (x, y, z), core


def device(c, core):
    x, y, z = c
    return ((x // 2) * 8 + y * 2 + core, z * 2 + lax.rem(x, 2))


def moved(c, axis, by):
    return c[:axis] + (lax.rem(c[axis] + 4 + by, 4),) + c[axis + 1 :]


def put(c, axis, value):
    return c[:axis] + (value,) + c[axis + 1 :]


def part(ref, c, rect, lead=()):
    x, y, z = c
    every = slice(None)
    xh, xl = (every, every) if x is None else (x // 2, lax.rem(x, 2))
    r0, nr, c0, nc = rect
    return ref.at[
        lead
        + (
            xh,
            every if y is None else y,
            every if z is None else z,
            xl,
            pl.ds(r0, nr),
            pl.ds(c0, nc),
        )
    ]


class Wire:
    def __init__(self, send_sem, recv_sem):
        self.send_sem, self.recv_sem, self.count, self.all = send_sem, recv_sem, 0, []

    def copy(self, src, dst, to):
        k = self.count
        self.count += 1
        made = pltpu.make_async_remote_copy(
            src_ref=src,
            dst_ref=dst,
            send_sem=self.send_sem.at[k],
            recv_sem=self.recv_sem.at[k],
            device_id=to,
            device_id_type=MESH,
        )
        self.all.append(made)
        return made

    def copies(self, src, src_c, dst, dst_c, rects, to, lead=()):
        return [
            self.copy(part(src, src_c, r, lead), part(dst, dst_c, r, lead), to)
            for r in rects
        ]


def start(copies):
    for c in copies:
        c.start()


def recv(copies):
    for c in copies:
        c.wait_recv()


def greet(devices):
    barrier = pltpu.get_barrier_semaphore()
    for d in devices:
        pl.semaphore_signal(barrier, inc=1, device_id=d, device_id_type=MESH)
    pl.semaphore_wait(barrier, len(devices))


def neighbours(me, core):
    near = [device(moved(me, a, s), core) for a in range(3) for s in (1, -1)]
    return near + [device(me, 1 - core)]


GATHER_COPIES = 3 * 2 * (18 + 4)


class Gather:
    def __init__(self, wire, full, me, core):
        d = 1 - 2 * core
        self.full, self.me, self.core = full, me, core
        partner = device(me, 1 - core)
        self.plan = []
        for (a1, a2, a3), rects in PIECES:
            t = {}

            def make(name, c, to):
                t[name] = wire.copies(full, c, full, c, rects, to, (core,))

            up = [device(moved(me, a, d), core) for a in (a1, a2, a3)]
            down = [device(moved(me, a, -d), core) for a in (a1, a2, a3)]
            make("1p", me, up[0])
            make("1m", me, down[0])
            make("1f", moved(me, a1, -d), up[0])
            row = put(me, a1, None)
            make("2p", row, up[1])
            make("2m", row, down[1])
            make("2f", moved(row, a2, -d), up[1])
            for j, by in enumerate((0, -d, d, 2)):
                line = moved(row, a2, by)
                make(f"3p{j}", line, up[2])
                make(f"3m{j}", line, down[2])
                make(f"3f{j}", moved(line, a3, -d), up[2])
            slab = put(row, a2, None)
            for j, by in enumerate((0, -d, d, 2)):
                make(f"x{j}", moved(slab, a3, by), partner)
            self.plan.append(t)

    def start(self):
        for t in self.plan:
            start(t["1p"] + t["1m"])

    def step1(self):
        for t in self.plan:
            recv(t["1p"])
            start(t["1f"])

    def step2(self):
        for t in self.plan:
            recv(t["1m"])
            recv(t["1f"])
            start(t["2p"] + t["2m"] + t["3p0"] + t["3m0"])

    def step3(self):
        for t in self.plan:
            recv(t["2p"])
            start(t["2f"] + t["3p1"] + t["3m1"])

    def step4(self):
        for t in self.plan:
            recv(t["2m"])
            start(t["3p2"] + t["3m2"])

    def step5(self):
        for t in self.plan:
            recv(t["2f"])
            start(t["3p3"] + t["3m3"] + t["x0"])

    def step6(self, j):
        for t in self.plan:
            recv(t[f"3p{j}"])
            start(t[f"3f{j}"])

    def step7(self):
        for t in self.plan:
            start(t["x1"])
        for t in self.plan:
            for j in range(4):
                recv(t[f"3m{j}"])
            start(t["x2"])

    def step8(self):
        for t in self.plan:
            for j in range(4):
                recv(t[f"3f{j}"])
            start(t["x3"])

    def step9(self):
        for j in range(4):
            for t in self.plan:
                recv(t[f"x{j}"])

    def run(self):
        self.start()
        self.step1()
        self.step2()
        self.step3()
        self.step4()
        self.step5()
        for j in range(4):
            self.step6(j)
        self.step7()
        self.step8()
        self.step9()


REDUCE_COPIES = 3 * 2 * 18


class Reduce:
    def __init__(self, wire, total, land, me, core):
        d = 1 - 2 * core
        self.total, self.land, self.me = total, land, me
        self.plan = []
        for (a1, a2, a3), rects in PIECES:
            t = {"rects": rects, "axes": (a1, a2, a3)}

            def make(name, src_c, dst_c, to):
                t[name] = wire.copies(total, src_c, land, dst_c, rects, to)

            up = [device(moved(me, a, d), core) for a in (a1, a2, a3)]
            down = [device(moved(me, a, -d), core) for a in (a1, a2, a3)]
            row = put(me, a1, None)
            t["lines"] = []
            for j, by in enumerate((2, -d, d, 0)):
                line = moved(row, a2, by)
                t["lines"].append(line)
                make(f"3x{j}", moved(line, a3, 2), moved(line, a3, 2), up[2])
                make(f"3m{j}", moved(line, a3, -d), moved(line, a3, 2), down[2])
                make(f"3p{j}", moved(line, a3, d), moved(line, a3, d), up[2])
            far = moved(row, a3, 2)
            make("2x", moved(row, a2, 2), moved(far, a2, 2), up[1])
            make("2m", moved(row, a2, -d), moved(far, a2, 2), down[1])
            make("2p", moved(row, a2, d), moved(far, a2, d), up[1])
            spot = moved(moved(me, a3, 2), a2, 2)
            make("1x", moved(me, a1, 2), moved(spot, a1, 2), up[0])
            make("1m", moved(me, a1, -d), moved(spot, a1, 2), down[0])
            make("1p", moved(me, a1, d), moved(spot, a1, d), up[0])
            t["d"], t["row"], t["far"], t["spot"] = d, row, far, spot
            self.plan.append(t)

    def add(self, t, where, sources):
        a1 = t["axes"][0]

        def one(c, sources_c):
            for r in t["rects"]:
                value = part(self.total, c, r)[...].astype(jnp.float32)
                for s in sources_c:
                    value = value + part(self.land, s, r)[...].astype(jnp.float32)
                part(self.total, c, r)[...] = value.astype(jnp.bfloat16)

        if where[a1] is None:

            @pl.loop(0, 4)
            def _(i):
                one(put(where, a1, i), [put(s, a1, i) for s in sources])

        else:
            one(where, sources)

    def start(self):
        for j in range(4):
            for t in self.plan:
                start(t[f"3x{j}"] + t[f"3m{j}"])

    def relay3(self, j):
        for t in self.plan:
            recv(t[f"3x{j}"])
            up = moved(t["lines"][j], t["axes"][2], t["d"])
            self.add(t, up, [up])
            start(t[f"3p{j}"])

    def close3(self, j):
        for t in self.plan:
            recv(t[f"3p{j}"])
            recv(t[f"3m{j}"])
            line, a3 = t["lines"][j], t["axes"][2]
            self.add(t, line, [line, moved(line, a3, -t["d"])])
            if j == 0:
                start(t["2x"])
            if j == 1:
                start(t["2m"])

    def relay2(self):
        for t in self.plan:
            recv(t["2x"])
            a2 = t["axes"][1]
            self.add(t, moved(t["row"], a2, t["d"]), [moved(t["far"], a2, t["d"])])
            start(t["2p"])

    def close2(self):
        for t in self.plan:
            recv(t["2p"])
            recv(t["2m"])
            a2 = t["axes"][1]
            self.add(t, t["row"], [t["far"], moved(t["far"], a2, -t["d"])])
            start(t["1x"] + t["1m"])

    def relay1(self):
        for t in self.plan:
            recv(t["1x"])
            a1 = t["axes"][0]
            self.add(t, moved(self.me, a1, t["d"]), [moved(t["spot"], a1, t["d"])])
            start(t["1p"])

    def close1(self, out):
        for t in self.plan:
            recv(t["1p"])
            recv(t["1m"])
            a1, d, spot = t["axes"][0], t["d"], t["spot"]
            for r in t["rects"]:
                value = part(self.total, self.me, r)[...].astype(jnp.float32)
                for s in (spot, moved(spot, a1, -d)):
                    value = value + part(self.land, s, r)[...].astype(jnp.float32)
                out[pl.ds(r[0], r[1]), pl.ds(r[2], r[3])] = value

    def run(self, out):
        self.start()
        for j in range(4):
            self.relay3(j)
        for j in range(3):
            self.close3(j)
        self.relay2()
        self.close3(3)
        self.close2()
        self.relay1()
        self.close1(out)


def tp_peers():
    rep, tp = lax.axis_index("rep"), lax.axis_index("tp")
    return [(rep, lax.rem(tp + k, 8)) for k in range(1, 8)]


def step_kernel(
    resid_hbm, cot_hbm, w_ref, gain_ref, smax_ref, ssum_ref, starg_ref, ids_ref, logp_ref, len_ref,
    value_ref, grad_hbm, wgrad_ref, ggrad_ref,
    full, resid, cot, inner, acc, squares, stage, cross, total, land, sums, grad, coef,
    stat_out, stat_in, part_out, part_in,
    g_send, g_recv, r_send, r_recv, x_send, x_recv, st_send, st_recv, pt_send, pt_recv,
    in_sem, cot_sem, out_sem,
):
    me, core = where_am_i()
    rep, tp = lax.axis_index("rep"), lax.axis_index("tp")
    x, y, z = me
    d_model = resid_hbm.shape[1]

    def load(k):
        return pltpu.make_async_copy(
            resid_hbm.at[:, pl.ds(pl.multiple_of(k * 512, 512), 512)], resid.at[k], in_sem.at[k]
        )

    for k in range(16):
        load(k).start()
    cot_load = pltpu.make_async_copy(cot_hbm, cot, cot_sem)
    cot_load.start()

    peers = tp_peers()
    near = neighbours(me, core)
    barrier = pltpu.get_barrier_semaphore()
    for to in near + peers:
        pl.semaphore_signal(barrier, inc=1, device_id=to, device_id_type=MESH)

    gain = jnp.broadcast_to(gain_ref[...].astype(jnp.float32), (128, 64)).T[:, 0:1]
    w = w_ref[...].astype(jnp.float32)
    full[core, x // 2, y, z, lax.rem(x, 2)] = (w * gain).astype(jnp.bfloat16)
    width = VOCAB // 8
    ids = ids_ref[...]
    mine = (ids >= tp * width) & (ids < (tp + 1) * width)
    owned = jnp.where(mine, starg_ref[...], 0.0)
    for k in range(8):
        cut = slice(k * 512, (k + 1) * 512)
        stat_out[k, :, 0:512] = smax_ref[:, cut]
        stat_out[k, :, 512:1024] = ssum_ref[:, cut]
        stat_out[k, :, 1024:1536] = owned[:, cut]
    pl.semaphore_wait(barrier, len(near) + len(peers))

    g_wire = Wire(g_send, g_recv)
    gather = Gather(g_wire, full, me, core)
    gather.start()
    stats = [
        pltpu.make_async_remote_copy(
            src_ref=stat_out.at[to[1]], dst_ref=stat_in.at[tp],
            send_sem=st_send.at[k], recv_sem=st_recv.at[k],
            device_id=to, device_id_type=MESH,
        )
        for k, to in enumerate(peers)
    ]
    start(stats)
    stat_in[tp] = stat_out[tp]

    squares[...] = jnp.zeros_like(squares)

    @pl.loop(0, 16)
    def _(k):
        load(k).wait()
        total_sq = squares[...]
        for i in range(4):
            part_x = resid[k, :, pl.ds(i * 128, 128)].astype(jnp.float32)
            total_sq = total_sq + part_x * part_x
        squares[...] = total_sq

        @pl.when(k == 12)
        def _():
            gather.step1()

    recv(stats)
    got = [stat_in[k] for k in range(8)]
    top = got[0][:, 0:512]
    for g in got[1:]:
        top = jnp.maximum(top, g[:, 0:512])
    sum_exp = jnp.zeros_like(top)
    picked = jnp.zeros_like(top)
    for g in got:
        sum_exp = sum_exp + g[:, 512:1024] * jnp.exp(g[:, 0:512] - top)
        picked = picked + g[:, 1024:1536]
    ref_logp = picked - top - jnp.log(sum_exp)
    length = len_ref[0, rep]
    spot = tp * 512 + lax.broadcasted_iota(jnp.int32, (1, 512), 1)
    live = (spot < length).astype(jnp.float32)
    local = jnp.sum(live * (logp_ref[...] - ref_logp), axis=1, keepdims=True)
    part_out[...] = jnp.broadcast_to(local, (8, 128))
    shares = [
        pltpu.make_async_remote_copy(
            src_ref=part_out, dst_ref=part_in.at[tp],
            send_sem=pt_send.at[k], recv_sem=pt_recv.at[k],
            device_id=to, device_id_type=MESH,
        )
        for k, to in enumerate(peers)
    ]
    start(shares)
    part_in[tp] = part_out[...]

    gather.step2()
    inv = lax.rsqrt(jnp.sum(squares[...], axis=1, keepdims=True) / d_model + EPS)
    rows = tp * 512 + lax.broadcasted_iota(jnp.int32, (512, 1), 0)
    live_rows = (rows < length).astype(jnp.float32)
    cot_load.wait()
    inner[...] = (cot[...].astype(jnp.float32) * (inv * live_rows)).astype(jnp.bfloat16)

    recv(shares)
    seq_total = part_in[0]
    for k in range(1, 8):
        seq_total = seq_total + part_in[k]
    delta = seq_total / jnp.full((8, 128), length, jnp.int32).astype(jnp.float32)
    seq_weight = (2.0 * jax.nn.sigmoid(BETA * delta) / 16.0)[0:1, 0:1]

    def g_chunk(r):
        g = lax.dot_general(
            resid[r], inner[...], (((0,), (0,)), ((), ())), preferred_element_type=jnp.float32
        )
        return g * seq_weight

    def across(i):
        return pltpu.make_async_remote_copy(
            src_ref=stage.at[i], dst_ref=cross.at[i],
            send_sem=x_send.at[i], recv_sem=x_recv.at[i],
            device_id=device(me, 1 - core), device_id_type=MESH,
        )

    @pl.loop(0, 8)
    def _(i):
        stage[i] = g_chunk(i * 2 + 1 - core).astype(jnp.bfloat16)
        across(i).start()
        for at, step in ((1, gather.step3), (3, gather.step4), (6, gather.step5)):

            @pl.when(i == at)
            def _():
                step()

    @pl.loop(0, 8)
    def _(i):
        mine = g_chunk(i * 2 + core)
        across(i).wait_recv()
        both = (mine + cross[i].astype(jnp.float32)).astype(jnp.bfloat16)
        total[i // 4, lax.rem(i, 4)] = both.reshape(4, 2, 64, 512)

    r_wire = Wire(r_send, r_recv)
    reduce = Reduce(r_wire, total, land, me, core)
    gather.step6(0)
    gather.step6(1)
    reduce.start()
    gather.step6(2)
    gather.step6(3)
    gather.step7()
    reduce.relay3(0)
    reduce.relay3(1)
    gather.step8()
    reduce.relay3(2)
    reduce.relay3(3)
    gather.step9()

    acc[...] = jnp.zeros_like(acc)

    def weight_chunk(k):
        return full[lax.rem(k, 2), k // 8, lax.rem(k // 2, 4)].reshape(512, 512)

    @pl.loop(0, 16)
    def _(k):
        acc[...] += jnp.dot(resid[k], weight_chunk(k), preferred_element_type=jnp.float32)
        for at, step in (
            (4, lambda: reduce.close3(0)),
            (8, lambda: reduce.close3(1)),
            (12, lambda: reduce.close3(2)),
        ):

            @pl.when(k == at)
            def _():
                step()

    value = acc[...] * inv
    value_ref[...] = value.astype(jnp.bfloat16)
    scale = live_rows * seq_weight
    mean = scale * (jnp.sum(cot[...].astype(jnp.float32) * value, axis=1, keepdims=True) / d_model)
    coef[0] = jnp.broadcast_to(inv * scale, (512, 128))
    coef[1] = jnp.broadcast_to(inv * inv * mean, (512, 128))

    def store(k, slot):
        return pltpu.make_async_copy(
            grad.at[slot], grad_hbm.at[:, pl.ds(pl.multiple_of(k * 512, 512), 512)], out_sem.at[slot]
        )

    @pl.loop(0, 16)
    def _(k):
        slot = lax.rem(k, 2)
        back = lax.dot_general(
            cot[...], weight_chunk(k), (((1,), (1,)), ((), ())), preferred_element_type=jnp.float32
        )

        @pl.when(k >= 2)
        def _():
            store(k, slot).wait()

        for i in range(4):
            cut = pl.ds(i * 128, 128)
            new = back[:, i * 128 : (i + 1) * 128] * coef[0] - resid[k, :, cut].astype(jnp.float32) * coef[1]
            grad[slot, :, cut] = new.astype(jnp.bfloat16)
        store(k, slot).start()
        for at, step in (
            (1, reduce.relay2),
            (5, lambda: reduce.close3(3)),
            (9, reduce.close2),
            (13, reduce.relay1),
        ):

            @pl.when(k == at)
            def _():
                step()

    reduce.close1(sums)
    summed = sums[...]
    wgrad_ref[...] = summed * gain
    gain_sum = jnp.sum(summed * w, axis=1, keepdims=True)
    ggrad_ref[...] = jnp.broadcast_to(gain_sum, (64, 128)).T[0:1, :]
    for slot in range(2):
        store(slot, slot).wait()

    @pl.loop(0, 8)
    def _(i):
        across(i).wait_send()

    for c in g_wire.all + r_wire.all + stats + shares:
        c.wait_send()


def per_device(
    residual, norm_gain, value_weight, value_cot, trainee_logp,
    ref_shard_max, ref_shard_sum, ref_target_logit, target_ids, lengths,
):
    vmem, anywhere = pl.BlockSpec(memory_space=pltpu.VMEM), pl.BlockSpec(memory_space=pl.ANY)
    dma = pltpu.SemaphoreType.DMA
    f32, bf16 = jnp.float32, jnp.bfloat16
    rows, d_model = residual.shape
    value, grad, wgrad, ggrad = pl.pallas_call(
        step_kernel,
        out_shape=(
            jax.ShapeDtypeStruct((rows, 512), bf16),
            jax.ShapeDtypeStruct((rows, d_model), bf16),
            jax.ShapeDtypeStruct((64, 512), f32),
            jax.ShapeDtypeStruct((1, 64), f32),
        ),
        in_specs=[anywhere, anywhere] + [vmem] * 7 + [pl.BlockSpec(memory_space=pltpu.SMEM)],
        out_specs=(vmem, anywhere, vmem, vmem),
        scratch_shapes=[
            pltpu.VMEM((2,) + CUBE + (64, 512), bf16),
            pltpu.VMEM((16, 512, 512), bf16),
            pltpu.VMEM((512, 512), bf16),
            pltpu.VMEM((512, 512), bf16),
            pltpu.VMEM((512, 512), f32),
            pltpu.VMEM((512, 128), f32),
            pltpu.VMEM((8, 512, 512), bf16),
            pltpu.VMEM((8, 512, 512), bf16),
            pltpu.VMEM(CUBE + (64, 512), bf16),
            pltpu.VMEM(CUBE + (64, 512), bf16),
            pltpu.VMEM((64, 512), f32),
            pltpu.VMEM((2, 512, 512), bf16),
            pltpu.VMEM((2, 512, 128), f32),
            pltpu.VMEM((8, 1, 1536), f32),
            pltpu.VMEM((8, 1, 1536), f32),
            pltpu.VMEM((8, 128), f32),
            pltpu.VMEM((8, 8, 128), f32),
            dma((GATHER_COPIES,)), dma((GATHER_COPIES,)),
            dma((REDUCE_COPIES,)), dma((REDUCE_COPIES,)),
            dma((8,)), dma((8,)),
            dma((7,)), dma((7,)), dma((7,)), dma((7,)),
            dma((16,)), dma, dma((2,)),
        ],
        compiler_params=pltpu.CompilerParams(
            collective_id=0, has_side_effects=True, vmem_limit_bytes=67_000_000
        ),
        name="step",
    )(
        residual, value_cot, value_weight, norm_gain.reshape(1, -1),
        ref_shard_max, ref_shard_sum, ref_target_logit,
        target_ids.reshape(1, -1), trainee_logp.reshape(1, -1), lengths.reshape(1, -1),
    )
    return value, grad, wgrad, ggrad.reshape(-1)


def solution(mesh):
    placed = (
        P(("rep", "tp"), None),
        P(("rep", "tp")),
        P(("rep", "tp"), None),
        P(("rep", "tp"), None),
        P(("rep", "tp")),
        P("tp", "rep"),
        P("tp", "rep"),
        P("tp", "rep"),
        P("rep"),
        P(),
    )
    return jax.shard_map(
        per_device,
        mesh=mesh,
        in_specs=placed,
        out_specs=(
            P(("rep", "tp"), None),
            P(("rep", "tp"), None),
            P(("rep", "tp"), None),
            P(("rep", "tp")),
        ),
        check_vma=False,
    )
```

```python
import jax
import jax.numpy as jnp
from jax import lax
from jax.experimental import pallas as pl
from jax.experimental.pallas import tpu as pltpu
from jax.sharding import PartitionSpec as P

VOCAB = 128256
EPS = 1e-05
BETA = 0.5
MESH = pl.DeviceIdType.MESH

PIECES = (((0, 1, 2), 0, 32), ((1, 2, 0), 32, 16), ((2, 0, 1), 48, 16))
HEIGHTS = tuple(64 + rows for _, _, rows in PIECES)
REDUCE_AXES = ((2, 0, 1), (0, 1, 2), (1, 2, 0))
CUBE = (2, 4, 4, 2)


def where_am_i():
    rep, tp = lax.axis_index("rep"), lax.axis_index("tp")
    core = lax.rem(rep, 2)
    y = lax.rem(rep // 2, 4)
    x = (rep // 8) * 2 + lax.rem(tp, 2)
    z = tp // 2
    return (x, y, z), core


def device(c, core):
    x, y, z = c
    return ((x // 2) * 8 + y * 2 + core, z * 2 + lax.rem(x, 2))


def moved(c, axis, by):
    return c[:axis] + (lax.rem(c[axis] + 4 + by, 4),) + c[axis + 1 :]


def put(c, axis, value):
    return c[:axis] + (value,) + c[axis + 1 :]


def part(ref, c, lead=()):
    x, y, z = c
    every = slice(None)
    xh, xl = (every, every) if x is None else (x // 2, lax.rem(x, 2))
    return ref.at[lead + (xh, every if y is None else y, every if z is None else z, xl)]


def scatter(refs, lead, block):
    for p, (_, first, rows) in enumerate(PIECES):
        refs[p].at[lead][..., 0:64, :] = block[..., p * 128 : (p + 1) * 128]
        refs[p].at[lead][..., 64 : 64 + rows, :] = block[..., first : first + rows, 384:512]


class Wire:
    def __init__(self, send_sem, recv_sem):
        self.send_sem, self.recv_sem, self.count, self.all = send_sem, recv_sem, 0, []

    def copy(self, src, dst, to):
        k = self.count
        self.count += 1
        made = pltpu.make_async_remote_copy(
            src_ref=src,
            dst_ref=dst,
            send_sem=self.send_sem.at[k],
            recv_sem=self.recv_sem.at[k],
            device_id=to,
            device_id_type=MESH,
        )
        self.all.append(made)
        return made


def start(copies):
    for c in copies:
        c.start()


def recv(copies):
    for c in copies:
        c.wait_recv()


def greet(devices):
    barrier = pltpu.get_barrier_semaphore()
    for d in devices:
        pl.semaphore_signal(barrier, inc=1, device_id=d, device_id_type=MESH)
    pl.semaphore_wait(barrier, len(devices))


def neighbours(me, core):
    near = [device(me, 1 - core)]
    for x in range(4):
        for y in range(4):
            for z in range(4):
                if 0 in (x, y, z) and (x, y, z) != (0, 0, 0):
                    near.append(device(moved(moved(moved(me, 0, x), 1, y), 2, z), core))
    return near


GATHER_COPIES = 3 * 31
LINES = (0, 1, 3, 2)


class Gather:
    def __init__(self, wire, full, me, core):
        d = 1 - 2 * core
        partner = device(me, 1 - core)
        self.plan = []
        for p, ((a1, a2, a3), _, _) in enumerate(PIECES):
            t = {}

            def make(name, c, to):
                place = part(full[p], c, (core,))
                t[name] = [wire.copy(place, place, to)]

            up, down = device(moved(me, a3, d), core), device(moved(me, a3, -d), core)
            row = put(me, a1, None)
            slab = put(row, a2, None)
            for j, by in enumerate(LINES):
                for k in LINES:
                    if (by, k) != (0, 0):
                        make(f"b{j}{k}", me, device(moved(moved(me, a1, k), a2, by), core))
                t[f"b{j}"] = [c for k in LINES if (by, k) != (0, 0) for c in t[f"b{j}{k}"]]
                line = moved(row, a2, -by)
                make(f"3p{j}", line, up)
                make(f"3m{j}", line, down)
                e, to = ((d, up), (-d, down))[j // 2]
                make(f"3f{j}", moved(line, a3, -e), to)
                make(f"x{j}", moved(slab, a3, (0, -d, d, 2)[j]), partner)
            self.plan.append(t)

    def start(self):
        for j in range(4):
            for t in self.plan:
                start(t[f"b{j}"])

    def line(self, j):
        for t in self.plan:
            recv(t[f"b{j}"])
            start(t[f"3p{j}"] + t[f"3m{j}"])

    def own(self):
        for t in self.plan:
            start(t["x0"])

    def far(self, j):
        for t in self.plan:
            recv(t[f"3p{j}" if j < 2 else f"3m{j}"])
            start(t[f"3f{j}"])

    def step7(self):
        for t in self.plan:
            recv(t["3p2"] + t["3p3"])
            start(t["x1"])
        for t in self.plan:
            recv(t["3m0"] + t["3m1"])
            start(t["x2"])

    def step8(self):
        for t in self.plan:
            for j in range(4):
                recv(t[f"3f{j}"])
            start(t["x3"])

    def step9(self):
        for j in range(4):
            for t in self.plan:
                recv(t[f"x{j}"])


REDUCE_COPIES = 3 * 27


class Reduce:
    def __init__(self, wire, total, land, me, core):
        d = 1 - 2 * core
        self.total, self.land, self.me, self.d = total, land, me, d
        self.plan = []
        for p, axes in enumerate(REDUCE_AXES):
            a1, a2, a3 = axes
            t = {"p": p, "axes": axes}

            def make(name, src_c, dst_c, to):
                t[name] = [wire.copy(part(total[p], src_c), part(land[p], dst_c), to)]

            up, down = device(moved(me, a3, d), core), device(moved(me, a3, -d), core)
            row = put(me, a1, None)
            spot = moved(me, a3, 2)
            t["lines"] = []
            for j, by in enumerate((2, -d, d, 0)):
                line = moved(row, a2, by)
                e, fore, back = ((d, up, down), (-d, down, up))[j % 2]
                t["lines"].append((line, e))
                make(f"3x{j}", moved(line, a3, 2), moved(line, a3, 2), fore)
                make(f"3m{j}", moved(line, a3, -e), moved(line, a3, 2), back)
                make(f"3p{j}", moved(line, a3, e), moved(line, a3, e), fore)
                for k in LINES:
                    if (j, k) != (3, 0):
                        to = moved(moved(me, a1, k), a2, by)
                        make(f"s{j}{k}", to, spot, device(to, core))
                t[f"s{j}"] = [c for k in LINES if (j, k) != (3, 0) for c in t[f"s{j}{k}"]]
            self.plan.append(t)

    def add(self, t, where, sources):
        a1, p = t["axes"][0], t["p"]

        def one(c, sources_c):
            value = part(self.total[p], c)[...].astype(jnp.float32)
            for s in sources_c:
                value = value + part(self.land[p], s)[...].astype(jnp.float32)
            part(self.total[p], c)[...] = value.astype(jnp.bfloat16)

        @pl.loop(0, 4)
        def _(i):
            one(put(where, a1, i), [put(s, a1, i) for s in sources])

    def send3(self, p, kinds, lines):
        for j in lines:
            for kind in kinds:
                start(self.plan[p][f"3{kind}{j}"])

    def relay3(self, j):
        for t in self.plan:
            recv(t[f"3x{j}"])
            line, e = t["lines"][j]
            up = moved(line, t["axes"][2], e)
            self.add(t, up, [up])
            start(t[f"3p{j}"])

    def close3(self, j):
        for t in self.plan:
            recv(t[f"3p{j}"])
            recv(t[f"3m{j}"])
            (line, e), a3 = t["lines"][j], t["axes"][2]
            self.add(t, line, [line, moved(line, a3, -e)])
            start(t[f"s{j}"])

    def finish(self, out):
        for t in self.plan:
            for j in range(4):
                recv(t[f"s{j}"])
            (a1, a2, a3), p = t["axes"], t["p"]
            spot = moved(self.me, a3, 2)
            part(self.land[p], spot)[...] = part(self.total[p], self.me)[...]
            value = jnp.zeros((HEIGHTS[p], 128), jnp.float32)
            for i in range(4):
                for k in range(4):
                    c = put(put(spot, a1, jnp.int32(i)), a2, jnp.int32(k))
                    value = value + part(self.land[p], c)[...].astype(jnp.float32)
            _, first, rows = PIECES[p]
            out[:, p * 128 : (p + 1) * 128] = value[0:64]
            out[first : first + rows, 384:512] = value[64:]


def tp_peers():
    rep, tp = lax.axis_index("rep"), lax.axis_index("tp")
    return [(rep, lax.rem(tp + k, 8)) for k in range(1, 8)]


def step_kernel(
    resid_hbm, cot_hbm, w_hbm, gain_hbm, smax_hbm, ssum_hbm, starg_hbm, ids_hbm, logp_hbm, len_hbm,
    value_ref, grad_ref, wgrad_ref, ggrad_ref,
    full_a, full_b, full_c, total_a, total_b, total_c, land_a, land_b, land_c,
    resid, cot, inner, acc, squares, stage, cross, sums, coef,
    w_ref, gain_ref, smax_ref, ssum_ref, starg_ref, ids_ref, logp_ref, len_ref,
    stat_out, stat_in, part_out, part_in,
    g_send, g_recv, r_send, r_recv, x_send, x_recv, st_send, st_recv, pt_send, pt_recv,
    in_sem, cot_sem, small_sem,
):
    me, core = where_am_i()
    rep, tp = lax.axis_index("rep"), lax.axis_index("tp")
    x, y, z = me
    d = 1 - 2 * core
    full, total, land = (full_a, full_b, full_c), (total_a, total_b, total_c), (land_a, land_b, land_c)
    d_model = resid_hbm.shape[1]

    def load(k):
        return pltpu.make_async_copy(
            resid_hbm.at[:, pl.ds(pl.multiple_of(k * 512, 512), 512)], resid.at[k], in_sem.at[k]
        )

    peers = tp_peers()
    near = neighbours(me, core)
    barrier = pltpu.get_barrier_semaphore()
    for to in near:
        pl.semaphore_signal(barrier, inc=1, device_id=to, device_id_type=MESH)
    small = [
        pltpu.make_async_copy(a, b, small_sem.at[k])
        for k, (a, b) in enumerate((
            (w_hbm, w_ref), (gain_hbm, gain_ref), (smax_hbm, smax_ref), (ssum_hbm, ssum_ref),
            (starg_hbm, starg_ref), (ids_hbm, ids_ref), (logp_hbm, logp_ref), (len_hbm, len_ref),
        ))
    ]
    start(small)
    for k in range(16):
        load(k).start()
    cot_load = pltpu.make_async_copy(cot_hbm, cot, cot_sem)
    cot_load.start()
    for c in small[0:2]:
        c.wait()
    gain = jnp.broadcast_to(gain_ref[...].astype(jnp.float32), (128, 64)).T[:, 0:1]
    w = w_ref[...].astype(jnp.float32)
    scatter(full, (core, x // 2, y, z, lax.rem(x, 2)), (w * gain).astype(jnp.bfloat16))
    pl.semaphore_wait(barrier, len(near))

    g_wire = Wire(g_send, g_recv)
    gather = Gather(g_wire, full, me, core)
    gather.start()
    for c in small[2:]:
        c.wait()
    width = VOCAB // 8
    ids = ids_ref[...]
    mine = (ids >= tp * width) & (ids < (tp + 1) * width)
    owned = jnp.where(mine, starg_ref[...], 0.0)
    for k in range(8):
        cut = slice(k * 512, (k + 1) * 512)
        stat_out[k, :, 0:512] = smax_ref[:, cut]
        stat_out[k, :, 512:1024] = ssum_ref[:, cut]
        stat_out[k, :, 1024:1536] = owned[:, cut]
    stats = [
        pltpu.make_async_remote_copy(
            src_ref=stat_out.at[to[1]], dst_ref=stat_in.at[tp],
            send_sem=st_send.at[k], recv_sem=st_recv.at[k],
            device_id=to, device_id_type=MESH,
        )
        for k, to in enumerate(peers)
    ]
    start(stats)
    stat_in[tp] = stat_out[tp]

    squares[...] = jnp.zeros_like(squares)

    @pl.loop(0, 16)
    def _(k):
        load(k).wait()
        total_sq = squares[...]
        for i in range(4):
            part_x = resid[k, :, pl.ds(i * 128, 128)].astype(jnp.float32)
            total_sq = total_sq + part_x * part_x
        squares[...] = total_sq

    recv(stats)
    got = [stat_in[k] for k in range(8)]
    top = got[0][:, 0:512]
    for g in got[1:]:
        top = jnp.maximum(top, g[:, 0:512])
    sum_exp = jnp.zeros_like(top)
    picked = jnp.zeros_like(top)
    for g in got:
        sum_exp = sum_exp + g[:, 512:1024] * jnp.exp(g[:, 0:512] - top)
        picked = picked + g[:, 1024:1536]
    ref_logp = picked - top - jnp.log(sum_exp)
    places = lax.broadcasted_iota(jnp.int32, (1, 16), 1)
    length = jnp.sum(jnp.where(places == rep, len_ref[...], 0), axis=1, keepdims=True)
    spot = tp * 512 + lax.broadcasted_iota(jnp.int32, (1, 512), 1)
    live = (spot < length).astype(jnp.float32)
    local = jnp.sum(live * (logp_ref[...] - ref_logp), axis=1, keepdims=True)
    part_out[...] = jnp.broadcast_to(local, (8, 128))
    shares = [
        pltpu.make_async_remote_copy(
            src_ref=part_out, dst_ref=part_in.at[tp],
            send_sem=pt_send.at[k], recv_sem=pt_recv.at[k],
            device_id=to, device_id_type=MESH,
        )
        for k, to in enumerate(peers)
    ]
    start(shares)
    part_in[tp] = part_out[...]

    gather.line(0)
    gather.line(1)
    inv = lax.rsqrt(jnp.sum(squares[...], axis=1, keepdims=True) / d_model + EPS)
    rows = tp * 512 + lax.broadcasted_iota(jnp.int32, (512, 1), 0)
    live_rows = (rows < length).astype(jnp.float32)
    cot_load.wait()
    inner[...] = (cot[...].astype(jnp.float32) * (inv * live_rows)).astype(jnp.bfloat16)

    recv(shares)
    seq_total = part_in[0]
    for k in range(1, 8):
        seq_total = seq_total + part_in[k]
    delta = seq_total / length.astype(jnp.float32)
    seq_weight = (2.0 * jax.nn.sigmoid(BETA * delta) / 16.0)[0:1, 0:1]

    def g_chunk(r):
        g = lax.dot_general(
            resid[r], inner[...], (((0,), (0,)), ((), ())), preferred_element_type=jnp.float32
        )
        return g * seq_weight

    def across(i):
        return pltpu.make_async_remote_copy(
            src_ref=stage.at[i], dst_ref=cross.at[i],
            send_sem=x_send.at[i], recv_sem=x_recv.at[i],
            device_id=device(me, 1 - core), device_id_type=MESH,
        )

    def order(i, sign):
        far_half = jnp.where((i == 0) | ((i >= 2) & (i <= 4)), 1, 0)
        late = jnp.where((i == 2) | (i == 5), 4 - sign, jnp.where((i == 3) | (i == 6), 4 + sign, 4))
        by = jnp.where(i < 2, 2, late)
        half = lax.rem(x // 2 + far_half, 2)
        return half, lax.rem(y + by, 4)

    r_wire = Wire(r_send, r_recv)
    reduce = Reduce(r_wire, total, land, me, core)

    @pl.loop(0, 9)
    def _(i):
        @pl.when(i < 8)
        def _():
            half, row = order(i, -d)
            stage[i] = g_chunk((half * 4 + row) * 2 + 1 - core).astype(jnp.bfloat16)
            across(i).start()

        @pl.when(i > 0)
        def _():
            half, row = order(i - 1, d)
            mine = g_chunk((half * 4 + row) * 2 + core)
            across(i - 1).wait_recv()
            both = (mine + cross[i - 1].astype(jnp.float32)).astype(jnp.bfloat16)
            scatter(total, (half, row), both.reshape(4, 2, 64, 512))

        for at, steps in (
            (1, (lambda: gather.line(2),)),
            (2, (lambda: gather.line(3), gather.own, lambda: reduce.send3(1, "xm", (0,)), lambda: reduce.send3(0, "x", range(4)))),
            (4, (lambda: gather.far(0),)),
            (5, (lambda: reduce.send3(2, "x", range(4)),)),
            (6, (lambda: gather.far(1), lambda: reduce.send3(1, "xm", (1,)), lambda: reduce.send3(0, "m", (0, 2)))),
            (7, (lambda: gather.far(2), lambda: reduce.send3(1, "xm", (2,)), lambda: reduce.send3(0, "m", (1, 3)))),
            (8, (lambda: reduce.send3(1, "xm", (3,)), lambda: reduce.send3(2, "m", range(4)))),
        ):

            @pl.when(i == at)
            def _():
                for step in steps:
                    step()

    gather.far(3)
    gather.step7()
    reduce.relay3(0)
    reduce.relay3(1)
    gather.step8()
    reduce.relay3(2)
    reduce.relay3(3)
    gather.step9()

    acc[...] = jnp.zeros_like(acc)

    def weight_chunk(k):
        at = (lax.rem(k, 2), k // 8, lax.rem(k // 2, 4))
        main = [full[p].at[at][..., 0:64, :].reshape(512, 128) for p in range(3)]
        rest = [full[p].at[at][..., 64 : HEIGHTS[p], :] for p in range(3)]
        return jnp.concatenate(main + [jnp.concatenate(rest, axis=2).reshape(512, 128)], axis=1)

    @pl.loop(0, 16)
    def _(k):
        acc[...] += jnp.dot(resid[k], weight_chunk(k), preferred_element_type=jnp.float32)
        for at, step in (
            (4, lambda: reduce.close3(0)),
            (8, lambda: reduce.close3(1)),
            (12, lambda: reduce.close3(2)),
        ):

            @pl.when(k == at)
            def _():
                step()

    value = acc[...] * inv
    value_ref[...] = value.astype(jnp.bfloat16)
    scale = live_rows * seq_weight
    mean = scale * (jnp.sum(cot[...].astype(jnp.float32) * value, axis=1, keepdims=True) / d_model)
    coef[0] = jnp.broadcast_to(inv * scale, (512, 128))
    coef[1] = jnp.broadcast_to(inv * inv * mean, (512, 128))

    @pl.loop(0, 16)
    def _(k):
        back = lax.dot_general(
            cot[...], weight_chunk(k), (((1,), (1,)), ((), ())), preferred_element_type=jnp.float32
        )

        for i in range(4):
            cut = pl.ds(i * 128, 128)
            new = back[:, i * 128 : (i + 1) * 128] * coef[0] - resid[k, :, cut].astype(jnp.float32) * coef[1]
            grad_ref[k, :, cut] = new.astype(jnp.bfloat16)
        for at, step in (
            (4, lambda: reduce.close3(3)),
        ):

            @pl.when(k == at)
            def _():
                step()

    reduce.finish(sums)
    summed = sums[...]
    wgrad_ref[...] = summed * gain
    gain_sum = jnp.sum(summed * w, axis=1, keepdims=True)
    ggrad_ref[...] = jnp.broadcast_to(gain_sum, (64, 128)).T[0:1, :]

    @pl.loop(0, 8)
    def _(i):
        across(i).wait_send()

    for c in g_wire.all + r_wire.all + stats + shares:
        c.wait_send()


def per_device(
    residual, norm_gain, value_weight, value_cot, trainee_logp,
    ref_shard_max, ref_shard_sum, ref_target_logit, target_ids, lengths,
):
    vmem, anywhere = pl.BlockSpec(memory_space=pltpu.VMEM), pl.BlockSpec(memory_space=pl.ANY)
    dma = pltpu.SemaphoreType.DMA
    f32, bf16 = jnp.float32, jnp.bfloat16
    rows, d_model = residual.shape
    value, grad, wgrad, ggrad = pl.pallas_call(
        step_kernel,
        out_shape=(
            pltpu.VMEM((rows, 512), bf16),
            pltpu.VMEM((16, 512, 512), bf16),
            pltpu.VMEM((64, 512), f32),
            pltpu.VMEM((1, 64), f32),
        ),
        in_specs=[anywhere] * 10,
        out_specs=(vmem, vmem, vmem, vmem),
        scratch_shapes=[
            *[pltpu.VMEM((2,) + CUBE + (h, 128), bf16) for h in HEIGHTS],
            *[pltpu.VMEM(CUBE + (h, 128), bf16) for h in HEIGHTS * 2],
            pltpu.VMEM((16, 512, 512), bf16),
            pltpu.VMEM((512, 512), bf16),
            pltpu.VMEM((512, 512), bf16),
            pltpu.VMEM((512, 512), f32),
            pltpu.VMEM((512, 128), f32),
            pltpu.VMEM((8, 512, 512), bf16),
            pltpu.VMEM((8, 512, 512), bf16),
            pltpu.VMEM((64, 512), f32),
            pltpu.VMEM((2, 512, 128), f32),
            pltpu.VMEM((64, 512), bf16),
            pltpu.VMEM((1, 64), bf16),
            *[pltpu.VMEM((1, 4096), f32)] * 3,
            pltpu.VMEM((1, 4096), jnp.int32),
            pltpu.VMEM((1, 512), f32),
            pltpu.VMEM((1, 16), jnp.int32),
            pltpu.VMEM((8, 1, 1536), f32),
            pltpu.VMEM((8, 1, 1536), f32),
            pltpu.VMEM((8, 128), f32),
            pltpu.VMEM((8, 8, 128), f32),
            dma((GATHER_COPIES,)), dma((GATHER_COPIES,)),
            dma((REDUCE_COPIES,)), dma((REDUCE_COPIES,)),
            dma((8,)), dma((8,)),
            dma((7,)), dma((7,)), dma((7,)), dma((7,)),
            dma((16,)), dma, dma((8,)),
        ],
        compiler_params=pltpu.CompilerParams(
            collective_id=0, has_side_effects=True, vmem_limit_bytes=57_950_000
        ),
        name="step",
    )(
        residual, value_cot, value_weight, norm_gain.reshape(1, -1),
        ref_shard_max, ref_shard_sum, ref_target_logit,
        target_ids.reshape(1, -1), trainee_logp.reshape(1, -1), lengths.reshape(1, -1),
    )
    def finish(v_in, g_in, w_in, a_in, v_out, g_out, w_out, a_out, sem):
        copies = [pltpu.make_async_copy(g_in.at[k], g_out.at[:, pl.ds(k * 512, 512)], sem.at[k]) for k in range(16)]
        copies += [pltpu.make_async_copy(a, b, sem.at[16 + i]) for i, (a, b) in enumerate(((v_in, v_out), (w_in, w_out), (a_in, a_out)))]
        for c in copies:
            c.start()
        for c in copies:
            c.wait()

    value, grad, wgrad, ggrad = pl.pallas_call(
        finish,
        out_shape=(
            jax.ShapeDtypeStruct((rows, 512), bf16),
            jax.ShapeDtypeStruct((rows, d_model), bf16),
            jax.ShapeDtypeStruct((64, 512), f32),
            jax.ShapeDtypeStruct((1, 64), f32),
        ),
        in_specs=[vmem] * 4,
        out_specs=[anywhere] * 4,
        scratch_shapes=[dma((19,))],
        compiler_params=pltpu.CompilerParams(vmem_limit_bytes=4_000_000),
        name="finish",
    )(value, grad, wgrad, ggrad)
    return value, grad, wgrad, ggrad.reshape(-1)


def solution(mesh):
    placed = (
        P(("rep", "tp"), None),
        P(("rep", "tp")),
        P(("rep", "tp"), None),
        P(("rep", "tp"), None),
        P(("rep", "tp")),
        P("tp", "rep"),
        P("tp", "rep"),
        P("tp", "rep"),
        P("rep"),
        P(),
    )
    return jax.shard_map(
        per_device,
        mesh=mesh,
        in_specs=placed,
        out_specs=(
            P(("rep", "tp"), None),
            P(("rep", "tp"), None),
            P(("rep", "tp"), None),
            P(("rep", "tp")),
        ),
        check_vma=False,
    )
```

```python
import jax
import jax.numpy as jnp
from jax import lax
from jax.experimental import pallas as pl
from jax.experimental.pallas import tpu as pltpu
from jax.sharding import PartitionSpec as P

VOCAB = 128256
EPS = 1e-05
BETA = 0.5
MESH = pl.DeviceIdType.MESH

PIECES = (((0, 1, 2), 0, 32), ((1, 2, 0), 32, 16), ((2, 0, 1), 48, 16))
HEIGHTS = tuple(64 + rows for _, _, rows in PIECES)
REDUCE_AXES = ((2, 0, 1), (0, 1, 2), (1, 2, 0))
CUBE = (2, 4, 4, 2)


def where_am_i():
    rep, tp = lax.axis_index("rep"), lax.axis_index("tp")
    core = lax.rem(rep, 2)
    y = lax.rem(rep // 2, 4)
    x = (rep // 8) * 2 + lax.rem(tp, 2)
    z = tp // 2
    return (x, y, z), core


def device(c, core):
    x, y, z = c
    return ((x // 2) * 8 + y * 2 + core, z * 2 + lax.rem(x, 2))


def moved(c, axis, by):
    return c[:axis] + (lax.rem(c[axis] + 4 + by, 4),) + c[axis + 1 :]


def put(c, axis, value):
    return c[:axis] + (value,) + c[axis + 1 :]


def part(ref, c, lead=()):
    x, y, z = c
    every = slice(None)
    spans = {None: every, "lo": pl.ds(0, 2), "hi": pl.ds(2, 2)}

    def span(v):
        return spans[v] if v is None or isinstance(v, str) else v

    if x is None:
        xh, xl = every, every
    elif isinstance(x, str):
        xh, xl = ("lo", "hi").index(x), every
    else:
        xh, xl = x // 2, lax.rem(x, 2)
    return ref.at[lead + (xh, span(y), span(z), xl)]


def scatter(refs, lead, block):
    for p, (_, first, rows) in enumerate(PIECES):
        refs[p].at[lead][..., 0:64, :] = block[..., p * 128 : (p + 1) * 128]
        refs[p].at[lead][..., 64 : 64 + rows, :] = block[..., first : first + rows, 384:512]


class Wire:
    def __init__(self, send_sem, recv_sem):
        self.send_sem, self.recv_sem, self.count, self.all = send_sem, recv_sem, 0, []

    def copy(self, src, dst, to):
        k = self.count
        self.count += 1
        made = pltpu.make_async_remote_copy(
            src_ref=src,
            dst_ref=dst,
            send_sem=self.send_sem.at[k],
            recv_sem=self.recv_sem.at[k],
            device_id=to,
            device_id_type=MESH,
        )
        self.all.append(made)
        return made


def start(copies):
    for c in copies:
        c.start()


def recv(copies):
    for c in copies:
        c.wait_recv()


def greet(devices):
    barrier = pltpu.get_barrier_semaphore()
    for d in devices:
        pl.semaphore_signal(barrier, inc=1, device_id=d, device_id_type=MESH)
    pl.semaphore_wait(barrier, len(devices))


def neighbours(me, core):
    ring = [device(moved(me, a, k), core) for a in range(3) for k in (1, 2, 3)]
    return [device(me, 1 - core)] + ring


GATHER_COPIES = 3 * 31


class Gather:
    def __init__(self, wire, full, me, core):
        d = 1 - 2 * core
        partner = device(me, 1 - core)
        self.plan = []
        for p, ((a1, a2, a3), _, _) in enumerate(PIECES):
            t = {}

            def make(name, c, to):
                place = part(full[p], c, (core,))
                t[name] = [wire.copy(place, place, to)]

            ups = [device(moved(me, a, d), core) for a in (a1, a2, a3)]
            downs = [device(moved(me, a, -d), core) for a in (a1, a2, a3)]
            row = put(me, a1, None)
            slab = put(row, a2, None)
            for u, k in enumerate((0, 1, 3, 2)):
                if u > 0:
                    make(f"1{u}", me, device(moved(me, a1, k), core))
                one = moved(me, a1, -k)
                make(f"2p{u}", one, ups[1])
                make(f"2m{u}", one, downs[1])
                e, to = ((d, ups[1]), (-d, downs[1]))[u // 2]
                make(f"2f{u}", moved(one, a2, -e), to)
            for j, by in enumerate((0, -d, d, 2)):
                line = moved(row, a2, by)
                make(f"3p{j}", line, ups[2])
                make(f"3m{j}", line, downs[2])
                e, to = ((d, ups[2]), (-d, downs[2]))[j // 2]
                make(f"3f{j}", moved(line, a3, -e), to)
                make(f"x{j}", moved(slab, a3, by), partner)
            self.plan.append(t)

    def start(self):
        for t in self.plan:
            start(t["11"] + t["12"] + t["13"])
        for t in self.plan:
            start(t["2p0"] + t["2m0"])

    def rows(self):
        for u in (1, 2, 3):
            for t in self.plan:
                recv(t[f"1{u}"])
                start(t[f"2p{u}"] + t[f"2m{u}"])

    def line0(self):
        for t in self.plan:
            start(t["3p0"] + t["3m0"])

    def relay(self):
        for u, name in ((0, "2p"), (2, "2m"), (1, "2p"), (3, "2m")):
            for t in self.plan:
                recv(t[f"{name}{u}"])
                start(t[f"2f{u}"])

    def lines(self):
        for t in self.plan:
            recv(t["2p2"] + t["2p3"])
            start(t["3p1"] + t["3m1"])
        for t in self.plan:
            recv(t["2m0"] + t["2m1"])
            start(t["3p2"] + t["3m2"])

    def line3(self):
        for t in self.plan:
            for u in range(4):
                recv(t[f"2f{u}"])
            start(t["3p3"] + t["3m3"])

    def own(self):
        for t in self.plan:
            start(t["x0"])

    def far(self, j):
        for t in self.plan:
            recv(t[f"3p{j}" if j < 2 else f"3m{j}"])
            start(t[f"3f{j}"])

    def step7(self):
        for t in self.plan:
            recv(t["3p2"] + t["3p3"])
            start(t["x1"])
        for t in self.plan:
            recv(t["3m0"] + t["3m1"])
            start(t["x2"])

    def step8(self):
        for t in self.plan:
            for j in range(4):
                recv(t[f"3f{j}"])
            start(t["x3"])

    def step9(self):
        for j in range(4):
            for t in self.plan:
                recv(t[f"x{j}"])


REDUCE_COPIES = 3 * 21


class Reduce:
    def __init__(self, wire, total, land, me, core):
        d = 1 - 2 * core
        self.total, self.land, self.me, self.d = total, land, me, d
        self.plan = []
        for p, axes in enumerate(REDUCE_AXES):
            a1, a2, a3 = axes
            t = {"p": p, "axes": axes}

            def make(name, src_c, dst_c, to):
                t[name] = [wire.copy(part(total[p], src_c), part(land[p], dst_c), to)]

            up, down = device(moved(me, a3, d), core), device(moved(me, a3, -d), core)
            row = put(me, a1, None)
            t["lines"] = []
            for j, by in enumerate((2, -d, d, 0)):
                line = moved(row, a2, by)
                e, fore, back = ((d, up, down), (-d, down, up))[j % 2]
                t["lines"].append((line, e))
                make(f"3x{j}", moved(line, a3, 2), moved(line, a3, 2), fore)
                make(f"3m{j}", moved(line, a3, -e), moved(line, a3, 2), back)
                make(f"3p{j}", moved(line, a3, e), moved(line, a3, e), fore)
            t["halves"] = []
            up, down = device(moved(me, a2, d), core), device(moved(me, a2, -d), core)
            for half, e, fore, back in (("lo", d, up, down), ("hi", -d, down, up)):
                near = put(me, a1, half)
                far = moved(near, a3, 2)
                t["halves"].append((half, near, far, e))
                make(f"2x{half}", moved(near, a2, 2), moved(far, a2, 2), fore)
                make(f"2m{half}", moved(near, a2, -e), moved(far, a2, 2), back)
                make(f"2p{half}", moved(near, a2, e), moved(far, a2, e), fore)
            t["spot"] = spot = moved(moved(me, a3, 2), a2, 2)
            for k in (1, 2, 3):
                make(f"1{k}", moved(me, a1, k), spot, device(moved(me, a1, k), core))
            self.plan.append(t)

    def add(self, t, where, sources):
        a1, p = t["axes"][0], t["p"]

        def one(c, sources_c):
            value = part(self.total[p], c)[...].astype(jnp.float32)
            for s in sources_c:
                value = value + part(self.land[p], s)[...].astype(jnp.float32)
            part(self.total[p], c)[...] = value.astype(jnp.bfloat16)

        first, last = {None: (0, 4), "lo": (0, 2), "hi": (2, 4)}[where[a1]]

        @pl.loop(first, last)
        def _(i):
            one(put(where, a1, i), [put(s, a1, i) for s in sources])

    def send3(self, p, kinds, lines):
        for j in lines:
            for kind in kinds:
                start(self.plan[p][f"3{kind}{j}"])

    def relay3(self, j):
        for t in self.plan:
            recv(t[f"3x{j}"])
            line, e = t["lines"][j]
            up = moved(line, t["axes"][2], e)
            self.add(t, up, [up])
            start(t[f"3p{j}"])

    def close3(self, j):
        for t in self.plan:
            recv(t[f"3p{j}"])
            recv(t[f"3m{j}"])
            (line, e), a3 = t["lines"][j], t["axes"][2]
            self.add(t, line, [line, moved(line, a3, -e)])
            if j < 3:
                start((t["2xlo"] + t["2xhi"], t["2mlo"], t["2mhi"])[j])

    def relay2(self):
        for t in self.plan:
            a2 = t["axes"][1]
            for half, near, far, e in t["halves"]:
                recv(t[f"2x{half}"])
                self.add(t, moved(near, a2, e), [moved(far, a2, e)])
                start(t[f"2p{half}"])

    def close2(self):
        for t in self.plan:
            a2 = t["axes"][1]
            for half, near, far, e in t["halves"]:
                recv(t[f"2p{half}"])
                recv(t[f"2m{half}"])
                self.add(t, near, [far, moved(far, a2, -e)])
            start(t["11"] + t["12"] + t["13"])

    def wait_sends(self, phases):
        for t in self.plan:
            for name, copies in t.items():
                if name[0] in phases:
                    for c in copies:
                        c.wait_send()

    def finish(self, out):
        for t in self.plan:
            a1, p = t["axes"][0], t["p"]
            value = part(self.total[p], self.me)[...].astype(jnp.float32)
            for k in (1, 2, 3):
                recv(t[f"1{k}"])
                value = value + part(self.land[p], moved(t["spot"], a1, 4 - k))[...].astype(jnp.float32)
            _, first, rows = PIECES[p]
            out[:, p * 128 : (p + 1) * 128] = value[0:64]
            out[first : first + rows, 384:512] = value[64:]


def tp_peers():
    rep, tp = lax.axis_index("rep"), lax.axis_index("tp")
    return [(rep, lax.rem(tp + k, 8)) for k in range(1, 8)]


def step_kernel(
    resid_hbm, cot_hbm, w_hbm, gain_hbm, smax_hbm, ssum_hbm, starg_hbm, ids_hbm, logp_hbm, len_hbm,
    value_ref, grad_ref, wgrad_ref, ggrad_ref,
    full_a, full_b, full_c, total_a, total_b, total_c, land_a, land_b, land_c,
    resid, cot, inner, acc, squares, stage, cross, sums, coef,
    w_ref, gain_ref, smax_ref, ssum_ref, starg_ref, ids_ref, logp_ref, len_ref,
    stat_out, stat_in, part_out, part_in,
    g_send, g_recv, r_send, r_recv, x_send, x_recv, st_send, st_recv, pt_send, pt_recv,
    in_sem, cot_sem, small_sem,
):
    me, core = where_am_i()
    rep, tp = lax.axis_index("rep"), lax.axis_index("tp")
    x, y, z = me
    d = 1 - 2 * core
    full, total, land = (full_a, full_b, full_c), (total_a, total_b, total_c), (land_a, land_b, land_c)
    d_model = resid_hbm.shape[1]

    def load(k):
        return pltpu.make_async_copy(
            resid_hbm.at[:, pl.ds(pl.multiple_of(k * 512, 512), 512)], resid.at[k], in_sem.at[k]
        )

    peers = tp_peers()
    near = neighbours(me, core)
    for k in (1, 2, 3):
        near.append(device((x - lax.rem(x, 2) + 1 - lax.rem(x, 2), y, lax.rem(z + k, 4)), core))
    barrier = pltpu.get_barrier_semaphore()
    for to in near:
        pl.semaphore_signal(barrier, inc=1, device_id=to, device_id_type=MESH)
    small = [
        pltpu.make_async_copy(a, b, small_sem.at[k])
        for k, (a, b) in enumerate((
            (w_hbm, w_ref), (gain_hbm, gain_ref), (smax_hbm, smax_ref), (ssum_hbm, ssum_ref),
            (starg_hbm, starg_ref), (ids_hbm, ids_ref), (logp_hbm, logp_ref), (len_hbm, len_ref),
        ))
    ]
    start(small)
    for k in range(16):
        load(k).start()
    cot_load = pltpu.make_async_copy(cot_hbm, cot, cot_sem)
    cot_load.start()
    for c in small[0:2]:
        c.wait()
    gain = jnp.broadcast_to(gain_ref[...].astype(jnp.float32), (128, 64)).T[:, 0:1]
    w = w_ref[...].astype(jnp.float32)
    scatter(full, (core, x // 2, y, z, lax.rem(x, 2)), (w * gain).astype(jnp.bfloat16))
    for c in small[2:]:
        c.wait()
    width = VOCAB // 8
    ids = ids_ref[...]
    mine = (ids >= tp * width) & (ids < (tp + 1) * width)
    owned = jnp.where(mine, starg_ref[...], 0.0)
    for k in range(8):
        cut = slice(k * 512, (k + 1) * 512)
        stat_out[k, :, 0:512] = smax_ref[:, cut]
        stat_out[k, :, 512:1024] = ssum_ref[:, cut]
        stat_out[k, :, 1024:1536] = owned[:, cut]
    pl.semaphore_wait(barrier, len(near))

    g_wire = Wire(g_send, g_recv)
    gather = Gather(g_wire, full, me, core)
    stats = [
        pltpu.make_async_remote_copy(
            src_ref=stat_out.at[to[1]], dst_ref=stat_in.at[tp],
            send_sem=st_send.at[k], recv_sem=st_recv.at[k],
            device_id=to, device_id_type=MESH,
        )
        for k, to in enumerate(peers)
    ]
    start(stats)
    gather.start()
    stat_in[tp] = stat_out[tp]

    squares[...] = jnp.zeros_like(squares)

    @pl.loop(0, 16)
    def _(k):
        load(k).wait()
        total_sq = squares[...]
        for i in range(4):
            part_x = resid[k, :, pl.ds(i * 128, 128)].astype(jnp.float32)
            total_sq = total_sq + part_x * part_x
        squares[...] = total_sq

        @pl.when(k == 10)
        def _():
            gather.rows()
            gather.line0()

    recv(stats)
    got = [stat_in[k] for k in range(8)]
    top = got[0][:, 0:512]
    for g in got[1:]:
        top = jnp.maximum(top, g[:, 0:512])
    sum_exp = jnp.zeros_like(top)
    picked = jnp.zeros_like(top)
    for g in got:
        sum_exp = sum_exp + g[:, 512:1024] * jnp.exp(g[:, 0:512] - top)
        picked = picked + g[:, 1024:1536]
    ref_logp = picked - top - jnp.log(sum_exp)
    places = lax.broadcasted_iota(jnp.int32, (1, 16), 1)
    length = jnp.sum(jnp.where(places == rep, len_ref[...], 0), axis=1, keepdims=True)
    spot = tp * 512 + lax.broadcasted_iota(jnp.int32, (1, 512), 1)
    live = (spot < length).astype(jnp.float32)
    local = jnp.sum(live * (logp_ref[...] - ref_logp), axis=1, keepdims=True)
    part_out[...] = jnp.broadcast_to(local, (8, 128))
    shares = [
        pltpu.make_async_remote_copy(
            src_ref=part_out, dst_ref=part_in.at[tp],
            send_sem=pt_send.at[k], recv_sem=pt_recv.at[k],
            device_id=to, device_id_type=MESH,
        )
        for k, to in enumerate(peers)
    ]
    start(shares)
    part_in[tp] = part_out[...]

    gather.relay()
    inv = lax.rsqrt(jnp.sum(squares[...], axis=1, keepdims=True) / d_model + EPS)
    rows = tp * 512 + lax.broadcasted_iota(jnp.int32, (512, 1), 0)
    live_rows = (rows < length).astype(jnp.float32)
    cot_load.wait()
    inner[...] = (cot[...].astype(jnp.float32) * (inv * live_rows)).astype(jnp.bfloat16)

    recv(shares)
    seq_total = part_in[0]
    for k in range(1, 8):
        seq_total = seq_total + part_in[k]
    delta = seq_total / length.astype(jnp.float32)
    seq_weight = (2.0 * jax.nn.sigmoid(BETA * delta) / 16.0)[0:1, 0:1]

    def g_chunk(r):
        g = lax.dot_general(
            resid[r], inner[...], (((0,), (0,)), ((), ())), preferred_element_type=jnp.float32
        )
        return g * seq_weight

    def across(i):
        return pltpu.make_async_remote_copy(
            src_ref=stage.at[i], dst_ref=cross.at[i],
            send_sem=x_send.at[i], recv_sem=x_recv.at[i],
            device_id=device(me, 1 - core), device_id_type=MESH,
        )

    def order(i, sign):
        far_half = jnp.where((i == 0) | ((i >= 2) & (i <= 4)), 1, 0)
        late = jnp.where((i == 2) | (i == 5), 4 - sign, jnp.where((i == 3) | (i == 6), 4 + sign, 4))
        by = jnp.where(i < 2, 2, late)
        half = lax.rem(x // 2 + far_half, 2)
        return half, lax.rem(y + by, 4)

    r_wire = Wire(r_send, r_recv)
    reduce = Reduce(r_wire, total, land, me, core)

    @pl.loop(0, 9)
    def _(i):
        @pl.when(i < 8)
        def _():
            half, row = order(i, -d)
            stage[i] = g_chunk((half * 4 + row) * 2 + 1 - core).astype(jnp.bfloat16)
            across(i).start()

        @pl.when(i > 0)
        def _():
            half, row = order(i - 1, d)
            mine = g_chunk((half * 4 + row) * 2 + core)
            across(i - 1).wait_recv()
            both = (mine + cross[i - 1].astype(jnp.float32)).astype(jnp.bfloat16)
            scatter(total, (half, row), both.reshape(4, 2, 64, 512))

        @pl.when(i == 0)
        def _():
            gather.lines()

        @pl.when(i == 2)
        def _():
            gather.far(0)

        @pl.when(i == 3)
        def _():
            gather.line3()
            gather.own()

        @pl.when(i == 5)
        def _():
            gather.far(1)

        @pl.when(i == 6)
        def _():
            gather.far(2)

        @pl.when(i == 8)
        def _():
            gather.far(3)
            reduce.send3(1, "xm", range(4))
            reduce.send3(0, "xm", range(4))
            reduce.send3(2, "xm", range(4))

    gather.step7()
    gather.step8()
    gather.step9()

    acc[...] = jnp.zeros_like(acc)

    def weight_chunk(k):
        at = (lax.rem(k, 2), k // 8, lax.rem(k // 2, 4))
        main = [full[p].at[at][..., 0:64, :].reshape(512, 128) for p in range(3)]
        rest = [full[p].at[at][..., 64 : HEIGHTS[p], :] for p in range(3)]
        return jnp.concatenate(main + [jnp.concatenate(rest, axis=2).reshape(512, 128)], axis=1)

    @pl.loop(0, 16)
    def _(k):
        acc[...] += jnp.dot(resid[k], weight_chunk(k), preferred_element_type=jnp.float32)
        @pl.when(k == 0)
        def _():
            reduce.relay3(0)

        @pl.when(k == 2)
        def _():
            reduce.relay3(1)

        @pl.when(k == 5)
        def _():
            reduce.relay3(2)

        @pl.when(k == 8)
        def _():
            reduce.relay3(3)

        @pl.when(k == 12)
        def _():
            reduce.close3(0)

        @pl.when(k == 14)
        def _():
            reduce.close3(1)

    value = acc[...] * inv
    value_ref[...] = value.astype(jnp.bfloat16)
    scale = live_rows * seq_weight
    mean = scale * (jnp.sum(cot[...].astype(jnp.float32) * value, axis=1, keepdims=True) / d_model)
    coef[0] = jnp.broadcast_to(inv * scale, (512, 128))
    coef[1] = jnp.broadcast_to(inv * inv * mean, (512, 128))

    @pl.loop(0, 16)
    def _(k):
        back = lax.dot_general(
            cot[...], weight_chunk(k), (((1,), (1,)), ((), ())), preferred_element_type=jnp.float32
        )

        for i in range(4):
            cut = pl.ds(i * 128, 128)
            new = back[:, i * 128 : (i + 1) * 128] * coef[0] - resid[k, :, cut].astype(jnp.float32) * coef[1]
            grad_ref[k, :, cut] = new.astype(jnp.bfloat16)
        @pl.when(k == 0)
        def _():
            reduce.close3(2)
            reduce.relay2()

        @pl.when(k == 3)
        def _():
            reduce.close3(3)

        @pl.when(k == 7)
        def _():
            reduce.close2()

    for c in g_wire.all + stats + shares:
        c.wait_send()

    @pl.loop(0, 8)
    def _(i):
        across(i).wait_send()

    reduce.wait_sends("32")
    reduce.finish(sums)
    summed = sums[...]
    wgrad_ref[...] = summed * gain
    gain_sum = jnp.sum(summed * w, axis=1, keepdims=True)
    ggrad_ref[...] = jnp.broadcast_to(gain_sum, (64, 128)).T[0:1, :]

    reduce.wait_sends("1")


def per_device(
    residual, norm_gain, value_weight, value_cot, trainee_logp,
    ref_shard_max, ref_shard_sum, ref_target_logit, target_ids, lengths,
):
    vmem, anywhere = pl.BlockSpec(memory_space=pltpu.VMEM), pl.BlockSpec(memory_space=pl.ANY)
    dma = pltpu.SemaphoreType.DMA
    f32, bf16 = jnp.float32, jnp.bfloat16
    rows, d_model = residual.shape
    value, grad, wgrad, ggrad = pl.pallas_call(
        step_kernel,
        out_shape=(
            pltpu.VMEM((rows, 512), bf16),
            pltpu.VMEM((16, 512, 512), bf16),
            pltpu.VMEM((64, 512), f32),
            pltpu.VMEM((1, 64), f32),
        ),
        in_specs=[anywhere] * 10,
        out_specs=(vmem, vmem, vmem, vmem),
        scratch_shapes=[
            *[pltpu.VMEM((2,) + CUBE + (h, 128), bf16) for h in HEIGHTS],
            *[pltpu.VMEM(CUBE + (h, 128), bf16) for h in HEIGHTS * 2],
            pltpu.VMEM((16, 512, 512), bf16),
            pltpu.VMEM((512, 512), bf16),
            pltpu.VMEM((512, 512), bf16),
            pltpu.VMEM((512, 512), f32),
            pltpu.VMEM((512, 128), f32),
            pltpu.VMEM((8, 512, 512), bf16),
            pltpu.VMEM((8, 512, 512), bf16),
            pltpu.VMEM((64, 512), f32),
            pltpu.VMEM((2, 512, 128), f32),
            pltpu.VMEM((64, 512), bf16),
            pltpu.VMEM((1, 64), bf16),
            *[pltpu.VMEM((1, 4096), f32)] * 3,
            pltpu.VMEM((1, 4096), jnp.int32),
            pltpu.VMEM((1, 512), f32),
            pltpu.VMEM((1, 16), jnp.int32),
            pltpu.VMEM((8, 1, 1536), f32),
            pltpu.VMEM((8, 1, 1536), f32),
            pltpu.VMEM((8, 128), f32),
            pltpu.VMEM((8, 8, 128), f32),
            dma((GATHER_COPIES,)), dma((GATHER_COPIES,)),
            dma((REDUCE_COPIES,)), dma((REDUCE_COPIES,)),
            dma((8,)), dma((8,)),
            dma((7,)), dma((7,)), dma((7,)), dma((7,)),
            dma((16,)), dma, dma((8,)),
        ],
        compiler_params=pltpu.CompilerParams(
            collective_id=0, has_side_effects=True, vmem_limit_bytes=57_950_000
        ),
        name="step",
    )(
        residual, value_cot, value_weight, norm_gain.reshape(1, -1),
        ref_shard_max, ref_shard_sum, ref_target_logit,
        target_ids.reshape(1, -1), trainee_logp.reshape(1, -1), lengths.reshape(1, -1),
    )
    def finish(v_in, g_in, w_in, a_in, v_out, g_out, w_out, a_out, sem):
        copies = [pltpu.make_async_copy(g_in.at[k], g_out.at[:, pl.ds(k * 512, 512)], sem.at[k]) for k in range(16)]
        copies += [pltpu.make_async_copy(a, b, sem.at[16 + i]) for i, (a, b) in enumerate(((v_in, v_out), (w_in, w_out), (a_in, a_out)))]
        for c in copies:
            c.start()
        for c in copies:
            c.wait()

    value, grad, wgrad, ggrad = pl.pallas_call(
        finish,
        out_shape=(
            jax.ShapeDtypeStruct((rows, 512), bf16),
            jax.ShapeDtypeStruct((rows, d_model), bf16),
            jax.ShapeDtypeStruct((64, 512), f32),
            jax.ShapeDtypeStruct((1, 64), f32),
        ),
        in_specs=[vmem] * 4,
        out_specs=[anywhere] * 4,
        scratch_shapes=[dma((19,))],
        compiler_params=pltpu.CompilerParams(vmem_limit_bytes=4_000_000),
        name="finish",
    )(value, grad, wgrad, ggrad)
    return value, grad, wgrad, ggrad.reshape(-1)


def solution(mesh):
    placed = (
        P(("rep", "tp"), None),
        P(("rep", "tp")),
        P(("rep", "tp"), None),
        P(("rep", "tp"), None),
        P(("rep", "tp")),
        P("tp", "rep"),
        P("tp", "rep"),
        P("tp", "rep"),
        P("rep"),
        P(),
    )
    return jax.shard_map(
        per_device,
        mesh=mesh,
        in_specs=placed,
        out_specs=(
            P(("rep", "tp"), None),
            P(("rep", "tp"), None),
            P(("rep", "tp"), None),
            P(("rep", "tp")),
        ),
        check_vma=False,
    )
```

```python
import jax
import jax.numpy as jnp
from jax import lax
from jax.experimental import pallas as pl
from jax.experimental.pallas import tpu as pltpu
from jax.sharding import PartitionSpec as P

VOCAB = 128256
EPS = 1e-05
BETA = 0.5
MESH = pl.DeviceIdType.MESH

PIECES = (((0, 1, 2), 0, 32), ((1, 2, 0), 32, 16), ((2, 0, 1), 48, 16))
HEIGHTS = tuple(64 + rows for _, _, rows in PIECES)
REDUCE_AXES = ((2, 0, 1), (0, 1, 2), (1, 2, 0))
CUBE = (2, 4, 4, 2)


def where_am_i():
    rep, tp = lax.axis_index("rep"), lax.axis_index("tp")
    core = lax.rem(rep, 2)
    y = lax.rem(rep // 2, 4)
    x = (rep // 8) * 2 + lax.rem(tp, 2)
    z = tp // 2
    return (x, y, z), core


def device(c, core):
    x, y, z = c
    return ((x // 2) * 8 + y * 2 + core, z * 2 + lax.rem(x, 2))


def moved(c, axis, by):
    return c[:axis] + (lax.rem(c[axis] + 4 + by, 4),) + c[axis + 1 :]


def put(c, axis, value):
    return c[:axis] + (value,) + c[axis + 1 :]


def part(ref, c, lead=()):
    x, y, z = c
    every = slice(None)
    spans = {None: every, "lo": pl.ds(0, 2), "hi": pl.ds(2, 2)}

    def span(v):
        return spans[v] if v is None or isinstance(v, str) else v

    if x is None:
        xh, xl = every, every
    elif isinstance(x, str):
        xh, xl = ("lo", "hi").index(x), every
    else:
        xh, xl = x // 2, lax.rem(x, 2)
    return ref.at[lead + (xh, span(y), span(z), xl)]


def scatter(refs, lead, block):
    for p, (_, first, rows) in enumerate(PIECES):
        refs[p].at[lead][..., 0:64, :] = block[..., p * 128 : (p + 1) * 128]
        refs[p].at[lead][..., 64 : 64 + rows, :] = block[..., first : first + rows, 384:512]


class Wire:
    def __init__(self, send_sem, recv_sem):
        self.send_sem, self.recv_sem, self.count, self.all = send_sem, recv_sem, 0, []

    def copy(self, src, dst, to):
        k = self.count
        self.count += 1
        made = pltpu.make_async_remote_copy(
            src_ref=src,
            dst_ref=dst,
            send_sem=self.send_sem.at[k],
            recv_sem=self.recv_sem.at[k],
            device_id=to,
            device_id_type=MESH,
        )
        self.all.append(made)
        return made


def start(copies):
    for c in copies:
        c.start()


def recv(copies):
    for c in copies:
        c.wait_recv()


def greet(devices):
    barrier = pltpu.get_barrier_semaphore()
    for d in devices:
        pl.semaphore_signal(barrier, inc=1, device_id=d, device_id_type=MESH)
    pl.semaphore_wait(barrier, len(devices))


def neighbours(me, core):
    ring = [device(moved(me, a, k), core) for a in range(3) for k in (1, 2, 3)]
    return [device(me, 1 - core)] + ring


GATHER_COPIES = 3 * 31


class Gather:
    def __init__(self, wire, full, me, core):
        d = 1 - 2 * core
        partner = device(me, 1 - core)
        self.plan = []
        for p, ((a1, a2, a3), _, _) in enumerate(PIECES):
            t = {}

            def make(name, c, to):
                place = part(full[p], c, (core,))
                t[name] = [wire.copy(place, place, to)]

            ups = [device(moved(me, a, d), core) for a in (a1, a2, a3)]
            downs = [device(moved(me, a, -d), core) for a in (a1, a2, a3)]
            row = put(me, a1, None)
            slab = put(row, a2, None)
            for u, k in enumerate((0, 1, 3, 2)):
                if u > 0:
                    make(f"1{u}", me, device(moved(me, a1, k), core))
                one = moved(me, a1, -k)
                make(f"2p{u}", one, ups[1])
                make(f"2m{u}", one, downs[1])
                e, to = ((d, ups[1]), (-d, downs[1]))[u // 2]
                make(f"2f{u}", moved(one, a2, -e), to)
            for j, by in enumerate((0, -d, d, 2)):
                line = moved(row, a2, by)
                make(f"3p{j}", line, ups[2])
                make(f"3m{j}", line, downs[2])
                e, to = ((d, ups[2]), (-d, downs[2]))[j // 2]
                make(f"3f{j}", moved(line, a3, -e), to)
                make(f"x{j}", moved(slab, a3, by), partner)
            self.plan.append(t)

    def start(self):
        for t in self.plan:
            start(t["11"] + t["12"] + t["13"])
        for t in self.plan:
            start(t["2p0"] + t["2m0"])

    def rows(self):
        for u in (1, 2, 3):
            for t in self.plan:
                recv(t[f"1{u}"])
                start(t[f"2p{u}"] + t[f"2m{u}"])

    def line0(self):
        for t in self.plan:
            start(t["3p0"] + t["3m0"])

    def relay(self):
        for u, name in ((0, "2p"), (2, "2m"), (1, "2p"), (3, "2m")):
            for t in self.plan:
                recv(t[f"{name}{u}"])
                start(t[f"2f{u}"])

    def lines(self):
        for t in self.plan:
            recv(t["2p2"] + t["2p3"])
            start(t["3p1"] + t["3m1"])
        for t in self.plan:
            recv(t["2m0"] + t["2m1"])
            start(t["3p2"] + t["3m2"])

    def line3(self):
        for t in self.plan:
            for u in range(4):
                recv(t[f"2f{u}"])
            start(t["3p3"] + t["3m3"])

    def own(self):
        for t in self.plan:
            start(t["x0"])

    def far(self, j):
        for t in self.plan:
            recv(t[f"3p{j}" if j < 2 else f"3m{j}"])
            start(t[f"3f{j}"])

    def step7(self):
        for t in self.plan:
            recv(t["3p2"] + t["3p3"])
            start(t["x1"])
        for t in self.plan:
            recv(t["3m0"] + t["3m1"])
            start(t["x2"])

    def step8(self):
        for t in self.plan:
            for j in range(4):
                recv(t[f"3f{j}"])
            start(t["x3"])

    def step9(self):
        for j in range(4):
            for t in self.plan:
                recv(t[f"x{j}"])


REDUCE_COPIES = 3 * 21


class Reduce:
    def __init__(self, wire, total, land, me, core):
        d = 1 - 2 * core
        self.total, self.land, self.me, self.d = total, land, me, d
        self.plan = []
        for p, axes in enumerate(REDUCE_AXES):
            a1, a2, a3 = axes
            t = {"p": p, "axes": axes}

            def make(name, src_c, dst_c, to):
                t[name] = [wire.copy(part(total[p], src_c), part(land[p], dst_c), to)]

            up, down = device(moved(me, a3, d), core), device(moved(me, a3, -d), core)
            row = put(me, a1, None)
            t["lines"] = []
            for j, by in enumerate((2, -d, d, 0)):
                line = moved(row, a2, by)
                e, fore, back = ((d, up, down), (-d, down, up))[j % 2]
                t["lines"].append((line, e))
                make(f"3x{j}", moved(line, a3, 2), moved(line, a3, 2), fore)
                make(f"3m{j}", moved(line, a3, -e), moved(line, a3, 2), back)
                make(f"3p{j}", moved(line, a3, e), moved(line, a3, e), fore)
            t["halves"] = []
            up, down = device(moved(me, a2, d), core), device(moved(me, a2, -d), core)
            for half, e, fore, back in (("lo", d, up, down), ("hi", -d, down, up)):
                near = put(me, a1, half)
                far = moved(near, a3, 2)
                t["halves"].append((half, near, far, e))
                make(f"2x{half}", moved(near, a2, 2), moved(far, a2, 2), fore)
                make(f"2m{half}", moved(near, a2, -e), moved(far, a2, 2), back)
                make(f"2p{half}", moved(near, a2, e), moved(far, a2, e), fore)
            t["spot"] = spot = moved(moved(me, a3, 2), a2, 2)
            for k in (1, 2, 3):
                make(f"1{k}", moved(me, a1, k), spot, device(moved(me, a1, k), core))
            self.plan.append(t)

    def add(self, t, where, sources):
        a1, p = t["axes"][0], t["p"]

        def one(c, sources_c):
            value = part(self.total[p], c)[...].astype(jnp.float32)
            for s in sources_c:
                value = value + part(self.land[p], s)[...].astype(jnp.float32)
            part(self.total[p], c)[...] = value.astype(jnp.bfloat16)

        first, last = {None: (0, 4), "lo": (0, 2), "hi": (2, 4)}[where[a1]]

        @pl.loop(first, last)
        def _(i):
            one(put(where, a1, i), [put(s, a1, i) for s in sources])

    def send3(self, p, kinds, lines):
        for j in lines:
            for kind in kinds:
                start(self.plan[p][f"3{kind}{j}"])

    def relay3(self, j):
        for t in self.plan:
            recv(t[f"3x{j}"])
            line, e = t["lines"][j]
            up = moved(line, t["axes"][2], e)
            self.add(t, up, [up])
            start(t[f"3p{j}"])

    def close3(self, j):
        for t in self.plan:
            recv(t[f"3p{j}"])
            recv(t[f"3m{j}"])
            (line, e), a3 = t["lines"][j], t["axes"][2]
            self.add(t, line, [line, moved(line, a3, -e)])
            if j < 3:
                start((t["2xlo"] + t["2xhi"], t["2mlo"], t["2mhi"])[j])

    def relay2(self):
        for t in self.plan:
            a2 = t["axes"][1]
            for half, near, far, e in t["halves"]:
                recv(t[f"2x{half}"])
                self.add(t, moved(near, a2, e), [moved(far, a2, e)])
                start(t[f"2p{half}"])

    def close2(self):
        for t in self.plan:
            a2 = t["axes"][1]
            for half, near, far, e in t["halves"]:
                recv(t[f"2p{half}"])
                recv(t[f"2m{half}"])
                self.add(t, near, [far, moved(far, a2, -e)])
            start(t["11"] + t["12"] + t["13"])

    def wait_sends(self, phases):
        for t in self.plan:
            for name, copies in t.items():
                if name[0] in phases:
                    for c in copies:
                        c.wait_send()

    def finish(self, out):
        for t in self.plan:
            a1, p = t["axes"][0], t["p"]
            value = part(self.total[p], self.me)[...].astype(jnp.float32)
            for k in (1, 2, 3):
                recv(t[f"1{k}"])
                value = value + part(self.land[p], moved(t["spot"], a1, 4 - k))[...].astype(jnp.float32)
            _, first, rows = PIECES[p]
            out[:, p * 128 : (p + 1) * 128] = value[0:64]
            out[first : first + rows, 384:512] = value[64:]


def tp_peers():
    rep, tp = lax.axis_index("rep"), lax.axis_index("tp")
    return [(rep, lax.rem(tp + k, 8)) for k in range(1, 8)]


def step_kernel(
    resid_hbm, cot_hbm, w_hbm, gain_hbm, smax_hbm, ssum_hbm, starg_hbm, ids_hbm, logp_hbm, len_hbm,
    value_ref, grad_ref, wgrad_ref, ggrad_ref,
    full_a, full_b, full_c, total_a, total_b, total_c, land_a, land_b, land_c,
    resid, cot, inner, acc, squares, stage, cross, sums, coef,
    w_ref, gain_ref, smax_ref, ssum_ref, starg_ref, ids_ref, logp_ref, len_ref,
    stat_out, stat_in, part_out, part_in,
    g_send, g_recv, r_send, r_recv, x_send, x_recv, st_send, st_recv, pt_send, pt_recv,
    in_sem, cot_sem, small_sem,
):
    me, core = where_am_i()
    rep, tp = lax.axis_index("rep"), lax.axis_index("tp")
    x, y, z = me
    d = 1 - 2 * core
    full, total, land = (full_a, full_b, full_c), (total_a, total_b, total_c), (land_a, land_b, land_c)
    d_model = resid_hbm.shape[1]

    def load(k):
        return pltpu.make_async_copy(
            resid_hbm.at[:, pl.ds(pl.multiple_of(k * 512, 512), 512)], resid.at[k], in_sem.at[k]
        )

    peers = tp_peers()
    near = neighbours(me, core)
    for k in (1, 2, 3):
        near.append(device((x - lax.rem(x, 2) + 1 - lax.rem(x, 2), y, lax.rem(z + k, 4)), core))
    barrier = pltpu.get_barrier_semaphore()
    for to in near:
        pl.semaphore_signal(barrier, inc=1, device_id=to, device_id_type=MESH)
    small = [
        pltpu.make_async_copy(a, b, small_sem.at[k])
        for k, (a, b) in enumerate((
            (w_hbm, w_ref), (gain_hbm, gain_ref), (smax_hbm, smax_ref), (ssum_hbm, ssum_ref),
            (starg_hbm, starg_ref), (ids_hbm, ids_ref), (logp_hbm, logp_ref), (len_hbm, len_ref),
        ))
    ]
    start(small)
    for k in range(16):
        load(k).start()
    cot_load = pltpu.make_async_copy(cot_hbm, cot, cot_sem)
    cot_load.start()
    for c in small[0:2]:
        c.wait()
    gain = jnp.broadcast_to(gain_ref[...].astype(jnp.float32), (128, 64)).T[:, 0:1]
    w = w_ref[...].astype(jnp.float32)
    scatter(full, (core, x // 2, y, z, lax.rem(x, 2)), (w * gain).astype(jnp.bfloat16))
    for c in small[2:]:
        c.wait()
    width = VOCAB // 8
    ids = ids_ref[...]
    mine = (ids >= tp * width) & (ids < (tp + 1) * width)
    owned = jnp.where(mine, starg_ref[...], 0.0)
    for k in range(8):
        cut = slice(k * 512, (k + 1) * 512)
        stat_out[k, :, 0:512] = smax_ref[:, cut]
        stat_out[k, :, 512:1024] = ssum_ref[:, cut]
        stat_out[k, :, 1024:1536] = owned[:, cut]
    pl.semaphore_wait(barrier, len(near))

    g_wire = Wire(g_send, g_recv)
    gather = Gather(g_wire, full, me, core)
    stats = [
        pltpu.make_async_remote_copy(
            src_ref=stat_out.at[to[1]], dst_ref=stat_in.at[tp],
            send_sem=st_send.at[k], recv_sem=st_recv.at[k],
            device_id=to, device_id_type=MESH,
        )
        for k, to in enumerate(peers)
    ]
    start(stats)
    gather.start()
    stat_in[tp] = stat_out[tp]

    squares[...] = jnp.zeros_like(squares)

    @pl.loop(0, 16)
    def _(k):
        load(k).wait()
        total_sq = squares[...]
        for i in range(4):
            part_x = resid[k, :, pl.ds(i * 128, 128)].astype(jnp.float32)
            total_sq = total_sq + part_x * part_x
        squares[...] = total_sq

        @pl.when(k == 6)
        def _():
            gather.rows()
            gather.line0()

    recv(stats)
    got = [stat_in[k] for k in range(8)]
    top = got[0][:, 0:512]
    for g in got[1:]:
        top = jnp.maximum(top, g[:, 0:512])
    sum_exp = jnp.zeros_like(top)
    picked = jnp.zeros_like(top)
    for g in got:
        sum_exp = sum_exp + g[:, 512:1024] * jnp.exp(g[:, 0:512] - top)
        picked = picked + g[:, 1024:1536]
    ref_logp = picked - top - jnp.log(sum_exp)
    places = lax.broadcasted_iota(jnp.int32, (1, 16), 1)
    length = jnp.sum(jnp.where(places == rep, len_ref[...], 0), axis=1, keepdims=True)
    spot = tp * 512 + lax.broadcasted_iota(jnp.int32, (1, 512), 1)
    live = (spot < length).astype(jnp.float32)
    local = jnp.sum(live * (logp_ref[...] - ref_logp), axis=1, keepdims=True)
    part_out[...] = jnp.broadcast_to(local, (8, 128))
    shares = [
        pltpu.make_async_remote_copy(
            src_ref=part_out, dst_ref=part_in.at[tp],
            send_sem=pt_send.at[k], recv_sem=pt_recv.at[k],
            device_id=to, device_id_type=MESH,
        )
        for k, to in enumerate(peers)
    ]
    start(shares)
    part_in[tp] = part_out[...]

    inv = lax.rsqrt(jnp.sum(squares[...], axis=1, keepdims=True) / d_model + EPS)
    rows = tp * 512 + lax.broadcasted_iota(jnp.int32, (512, 1), 0)
    live_rows = (rows < length).astype(jnp.float32)
    cot_load.wait()
    inner[...] = (cot[...].astype(jnp.float32) * (inv * live_rows)).astype(jnp.bfloat16)

    gather.relay()
    recv(shares)
    seq_total = part_in[0]
    for k in range(1, 8):
        seq_total = seq_total + part_in[k]
    delta = seq_total / length.astype(jnp.float32)
    seq_weight = (2.0 * jax.nn.sigmoid(BETA * delta) / 16.0)[0:1, 0:1]

    def g_chunk(r):
        g = lax.dot_general(
            resid[r], inner[...], (((0,), (0,)), ((), ())), preferred_element_type=jnp.float32
        )
        return g * seq_weight

    def across(i):
        return pltpu.make_async_remote_copy(
            src_ref=stage.at[i], dst_ref=cross.at[i],
            send_sem=x_send.at[i], recv_sem=x_recv.at[i],
            device_id=device(me, 1 - core), device_id_type=MESH,
        )

    def order(i, sign):
        far_half = jnp.where((i == 0) | ((i >= 2) & (i <= 4)), 1, 0)
        late = jnp.where((i == 2) | (i == 5), 4 - sign, jnp.where((i == 3) | (i == 6), 4 + sign, 4))
        by = jnp.where(i < 2, 2, late)
        half = lax.rem(x // 2 + far_half, 2)
        return half, lax.rem(y + by, 4)

    r_wire = Wire(r_send, r_recv)
    reduce = Reduce(r_wire, total, land, me, core)

    @pl.loop(0, 9)
    def _(i):
        @pl.when(i < 8)
        def _():
            half, row = order(i, -d)
            stage[i] = g_chunk((half * 4 + row) * 2 + 1 - core).astype(jnp.bfloat16)
            across(i).start()

        @pl.when(i > 0)
        def _():
            half, row = order(i - 1, d)
            mine = g_chunk((half * 4 + row) * 2 + core)
            across(i - 1).wait_recv()
            both = (mine + cross[i - 1].astype(jnp.float32)).astype(jnp.bfloat16)
            scatter(total, (half, row), both.reshape(4, 2, 64, 512))

        @pl.when(i == 0)
        def _():
            gather.lines()

        @pl.when(i == 2)
        def _():
            gather.far(0)

        @pl.when(i == 3)
        def _():
            gather.line3()
            gather.own()

        @pl.when(i == 5)
        def _():
            gather.far(1)

        @pl.when(i == 6)
        def _():
            gather.far(2)

        @pl.when(i == 8)
        def _():
            gather.far(3)
            reduce.send3(1, "xm", range(4))
            reduce.send3(0, "xm", range(4))
            reduce.send3(2, "xm", range(4))

    gather.step7()
    gather.step8()
    gather.step9()

    acc[...] = jnp.zeros_like(acc)

    def weight_chunk(k):
        at = (lax.rem(k, 2), k // 8, lax.rem(k // 2, 4))
        main = [full[p].at[at][..., 0:64, :].reshape(512, 128) for p in range(3)]
        rest = [full[p].at[at][..., 64 : HEIGHTS[p], :] for p in range(3)]
        return jnp.concatenate(main + [jnp.concatenate(rest, axis=2).reshape(512, 128)], axis=1)

    @pl.loop(0, 16)
    def _(k):
        acc[...] += jnp.dot(resid[k], weight_chunk(k), preferred_element_type=jnp.float32)
        @pl.when(k == 1)
        def _():
            reduce.relay3(0)

        @pl.when(k == 3)
        def _():
            reduce.relay3(1)

        @pl.when(k == 6)
        def _():
            reduce.relay3(2)

        @pl.when(k == 9)
        def _():
            reduce.relay3(3)

        @pl.when(k == 13)
        def _():
            reduce.close3(0)

        @pl.when(k == 15)
        def _():
            reduce.close3(1)

    value = acc[...] * inv
    value_ref[...] = value.astype(jnp.bfloat16)
    scale = live_rows * seq_weight
    mean = scale * (jnp.sum(cot[...].astype(jnp.float32) * value, axis=1, keepdims=True) / d_model)
    coef[0] = jnp.broadcast_to(inv * scale, (512, 128))
    coef[1] = jnp.broadcast_to(inv * inv * mean, (512, 128))

    @pl.loop(0, 16)
    def _(k):
        back = lax.dot_general(
            cot[...], weight_chunk(k), (((1,), (1,)), ((), ())), preferred_element_type=jnp.float32
        )

        for i in range(4):
            cut = pl.ds(i * 128, 128)
            new = back[:, i * 128 : (i + 1) * 128] * coef[0] - resid[k, :, cut].astype(jnp.float32) * coef[1]
            grad_ref[k, :, cut] = new.astype(jnp.bfloat16)
        @pl.when(k == 1)
        def _():
            reduce.close3(2)
            reduce.relay2()

        @pl.when(k == 4)
        def _():
            reduce.close3(3)

        @pl.when(k == 8)
        def _():
            reduce.close2()

    for c in g_wire.all + stats + shares:
        c.wait_send()

    @pl.loop(0, 8)
    def _(i):
        across(i).wait_send()

    reduce.wait_sends("32")
    reduce.finish(sums)
    summed = sums[...]
    wgrad_ref[...] = summed * gain
    gain_sum = jnp.sum(summed * w, axis=1, keepdims=True)
    ggrad_ref[...] = jnp.broadcast_to(gain_sum, (64, 128)).T[0:1, :]

    reduce.wait_sends("1")


def per_device(
    residual, norm_gain, value_weight, value_cot, trainee_logp,
    ref_shard_max, ref_shard_sum, ref_target_logit, target_ids, lengths,
):
    vmem, anywhere = pl.BlockSpec(memory_space=pltpu.VMEM), pl.BlockSpec(memory_space=pl.ANY)
    dma = pltpu.SemaphoreType.DMA
    f32, bf16 = jnp.float32, jnp.bfloat16
    rows, d_model = residual.shape
    value, grad, wgrad, ggrad = pl.pallas_call(
        step_kernel,
        out_shape=(
            pltpu.VMEM((rows, 512), bf16),
            pltpu.VMEM((16, 512, 512), bf16),
            pltpu.VMEM((64, 512), f32),
            pltpu.VMEM((1, 64), f32),
        ),
        in_specs=[anywhere] * 10,
        out_specs=(vmem, vmem, vmem, vmem),
        scratch_shapes=[
            *[pltpu.VMEM((2,) + CUBE + (h, 128), bf16) for h in HEIGHTS],
            *[pltpu.VMEM(CUBE + (h, 128), bf16) for h in HEIGHTS * 2],
            pltpu.VMEM((16, 512, 512), bf16),
            pltpu.VMEM((512, 512), bf16),
            pltpu.VMEM((512, 512), bf16),
            pltpu.VMEM((512, 512), f32),
            pltpu.VMEM((512, 128), f32),
            pltpu.VMEM((8, 512, 512), bf16),
            pltpu.VMEM((8, 512, 512), bf16),
            pltpu.VMEM((64, 512), f32),
            pltpu.VMEM((2, 512, 128), f32),
            pltpu.VMEM((64, 512), bf16),
            pltpu.VMEM((1, 64), bf16),
            *[pltpu.VMEM((1, 4096), f32)] * 3,
            pltpu.VMEM((1, 4096), jnp.int32),
            pltpu.VMEM((1, 512), f32),
            pltpu.VMEM((1, 16), jnp.int32),
            pltpu.VMEM((8, 1, 1536), f32),
            pltpu.VMEM((8, 1, 1536), f32),
            pltpu.VMEM((8, 128), f32),
            pltpu.VMEM((8, 8, 128), f32),
            dma((GATHER_COPIES,)), dma((GATHER_COPIES,)),
            dma((REDUCE_COPIES,)), dma((REDUCE_COPIES,)),
            dma((8,)), dma((8,)),
            dma((7,)), dma((7,)), dma((7,)), dma((7,)),
            dma((16,)), dma, dma((8,)),
        ],
        compiler_params=pltpu.CompilerParams(
            collective_id=0, has_side_effects=True, vmem_limit_bytes=57_950_000
        ),
        name="step",
    )(
        residual, value_cot, value_weight, norm_gain.reshape(1, -1),
        ref_shard_max, ref_shard_sum, ref_target_logit,
        target_ids.reshape(1, -1), trainee_logp.reshape(1, -1), lengths.reshape(1, -1),
    )
    def finish(v_in, g_in, w_in, a_in, v_out, g_out, w_out, a_out, sem):
        copies = [pltpu.make_async_copy(g_in.at[k], g_out.at[:, pl.ds(k * 512, 512)], sem.at[k]) for k in range(16)]
        copies += [pltpu.make_async_copy(a, b, sem.at[16 + i]) for i, (a, b) in enumerate(((v_in, v_out), (w_in, w_out), (a_in, a_out)))]
        for c in copies:
            c.start()
        for c in copies:
            c.wait()

    value, grad, wgrad, ggrad = pl.pallas_call(
        finish,
        out_shape=(
            jax.ShapeDtypeStruct((rows, 512), bf16),
            jax.ShapeDtypeStruct((rows, d_model), bf16),
            jax.ShapeDtypeStruct((64, 512), f32),
            jax.ShapeDtypeStruct((1, 64), f32),
        ),
        in_specs=[vmem] * 4,
        out_specs=[anywhere] * 4,
        scratch_shapes=[dma((19,))],
        compiler_params=pltpu.CompilerParams(vmem_limit_bytes=4_000_000),
        name="finish",
    )(value, grad, wgrad, ggrad)
    return value, grad, wgrad, ggrad.reshape(-1)


def solution(mesh):
    placed = (
        P(("rep", "tp"), None),
        P(("rep", "tp")),
        P(("rep", "tp"), None),
        P(("rep", "tp"), None),
        P(("rep", "tp")),
        P("tp", "rep"),
        P("tp", "rep"),
        P("tp", "rep"),
        P("rep"),
        P(),
    )
    return jax.shard_map(
        per_device,
        mesh=mesh,
        in_specs=placed,
        out_specs=(
            P(("rep", "tp"), None),
            P(("rep", "tp"), None),
            P(("rep", "tp"), None),
            P(("rep", "tp")),
        ),
        check_vma=False,
    )
```
